32 devices in a mesh: grp: 2 (over x), beam: 16 (over z, y, core).
Axes of the slice: x: 2, y: 2, z: 4, core: 2. Of those that a mesh axis runs over, the one named last changes fastest.
Arguments:
- hidden: bfloat16 [3, 64, 8192], P(None, ('grp', 'beam')), parts along dimension 1, may hold values from -6 to 6
- norm_gain: float32 [8192], replicated, may hold values from 0.5 to 1.5
- q_weight: bfloat16 [8192, 8192], P(None, 'beam'), may hold values from -0.0625 to 0.0625
- q_bias: float32 [8192], P('beam'), may hold values from -3 to 3
- kv_weight: bfloat16 [8192, 2, 1024], P(None, None, 'beam'), may hold values from -0.0625 to 0.0625
- kv_bias: float32 [2, 1024], P(None, 'beam'), may hold values from -5 to 5
- o_weight: bfloat16 [8192, 8192], P(None, 'beam'), may hold values from -0.0625 to 0.0625
- prefix_key_cache: bfloat16 [8, 2048, 1024], P('grp', 'beam'), parts along dimension 0, may hold values from -100 to 100
- prefix_value_cache: bfloat16 [8, 2048, 1024], P('grp', 'beam'), parts along dimension 0, may hold values from -12 to 12
- prefix_index: int32 [4], P('grp'), parts along dimension 0, may hold values from 0 to 3
- prefix_lens: int32 [4], P('grp'), parts along dimension 0, may hold values from 8 to 2048, as said below
- tail_key_cache: bfloat16 [64, 256, 1024], P(('grp', 'beam')), parts along dimension 0, may hold values from -12 to 12
- tail_value_cache: bfloat16 [64, 256, 1024], P(('grp', 'beam')), parts along dimension 0, may hold values from -12 to 12
- tail_lens: int32 [64], P('grp'), parts along dimension 0, may hold values from 1 to 256, as said below
- parents: int32 [3, 64], P(None, 'grp'), parts along dimension 1, may hold values from 0 to 31, as said below
Outputs:
- out: bfloat16 [3, 64, 8192], P(None, 'grp', 'beam'), parts along dimension 1
The draws below stay inside these ranges and needn't reach their ends.
There are 2 independent parts, one for each index of `grp`. The reference program is written for one: setup_inputs(seed, part) draws one part's arguments, and reference() takes and returns one part's arrays. A program takes and returns all parts, laid end to end along the dimension named above; an argument that names none is the same for every part. Nothing has to cross between parts.
Inputs may be any that keep to these rules, and one draw needn't show every extreme that they name: `prefix_lens`: the shared prefix lengths; some prompt uses all 2048 positions. `tail_lens`: the tail lengths; some row fills all 256 positions. parents[t, r] is one of the 16 rows of r's prompt: from r - r % 16 to r - r % 16 + 15.
All inputs are finite; a program needn't handle non-finite values.
Results may differ from the reference program's by a relative error of at most 0.012.
The reference program's roundings to bfloat16 on the way count: a program that leaves them out, or rounds other values in their place, can miss the bound.
Values may be sent and summed in bfloat16 or wider, within the bound.
A program may use at most 192 MiB of HBM per device.

```python
import math
import jax
import jax.numpy as jnp
import numpy as np
from jax import lax

D = 8192
QUERY_HEADS = 64
KEY_HEADS = 8
HEAD_DIM = 128
BEAM_COUNT = 16
STEPS = 3
NPREF = 4
ROW_DEV = 2
PREFIX_PER_CHIP = 128
TAIL_LENGTH = 256
QW = 8192
KVW = 1024
GROUP_SIZE = 8
BEAM_ROWS = 32
PROMPTS = 2
PREFIX_LENGTH = 2048


def draw_prefix_key_cache(key, part):
    first_key = jax.random.fold_in(key, 0)
    base = jnp.clip(2.0 * jax.random.normal(first_key, (NPREF, PREFIX_LENGTH, KVW), jnp.float32), -12.0, 12.0)
    return base.astype(jnp.bfloat16)


def draw_prefix_index(key, part):
    order = jax.random.permutation(jax.random.fold_in(key, 17), NPREF).astype(jnp.int32)
    return order[jnp.arange(PROMPTS, dtype=jnp.int32) % NPREF].astype(jnp.int32)


def draw_prefix_lens(key, part):
    base_key = jax.random.fold_in(jax.random.fold_in(key, 4211), part)
    long_key = jax.random.fold_in(base_key, 1)
    short_key = jax.random.fold_in(base_key, 2)
    pick_key = jax.random.fold_in(base_key, 3)
    full_key = jax.random.fold_in(base_key, 4)
    short_top = min(17, PREFIX_LENGTH + 1)
    long_lens = jax.random.randint(long_key, (PROMPTS,), 8, PREFIX_LENGTH + 1).astype(jnp.int32)
    short_lens = jax.random.randint(short_key, (PROMPTS,), 8, short_top).astype(jnp.int32)
    pick = jax.random.randint(pick_key, (PROMPTS,), 0, 2).astype(jnp.int32)
    full = jax.random.randint(full_key, (), 0, PROMPTS).astype(jnp.int32)
    prompt_ids = jnp.arange(PROMPTS, dtype=jnp.int32)
    forced_short = prompt_ids == (full + 1) % PROMPTS
    lengths = jnp.where((pick == 1) | forced_short, short_lens, long_lens)
    return jnp.where(prompt_ids == full, PREFIX_LENGTH, lengths).astype(jnp.int32)


def draw_tail_lens(key, part):
    length_key = jax.random.fold_in(key, 31)
    short_key = jax.random.fold_in(key, 32)
    pick_key = jax.random.fold_in(key, 33)
    full_key = jax.random.fold_in(key, 34)
    long_lens = jax.random.randint(length_key, (BEAM_ROWS,), 1, TAIL_LENGTH + 1).astype(jnp.int32)
    short_lens = jax.random.randint(short_key, (BEAM_ROWS,), 1, min(5, TAIL_LENGTH + 1)).astype(jnp.int32)
    pick = jax.random.randint(pick_key, (BEAM_ROWS,), 0, 2).astype(jnp.int32)
    lengths = jnp.where(pick == 1, short_lens, long_lens)
    full = jax.random.randint(full_key, (), 0, BEAM_ROWS).astype(jnp.int32)
    return jnp.where(jnp.arange(BEAM_ROWS, dtype=jnp.int32) == full, TAIL_LENGTH, lengths).astype(jnp.int32)


def draw_parents(key, part):
    starts = jnp.arange(BEAM_ROWS, dtype=jnp.int32) // BEAM_COUNT * BEAM_COUNT
    offsets = jax.random.randint(key, (STEPS, BEAM_ROWS), 0, BEAM_COUNT)
    return (starts[None, :] + offsets).astype(jnp.int32)


def block_levels(key, extent, shards, least, high):
    def one(axis_at, parts):
        draws = jax.random.uniform(jax.random.fold_in(jax.random.fold_in(key, 6), axis_at), (parts,), jnp.float32, least / len(shards), high / len(shards))
        return jnp.repeat(jnp.exp(draws), extent[axis_at] // parts).reshape((-1,) + (1,) * (len(extent) - axis_at - 1))

    loudness = one(*shards[0])
    for cut in shards[1:]:
        loudness = loudness * one(*cut)
    return loudness


def bell_draw(key, dims, deviation, bound, cuts=(), held_as=jnp.bfloat16):
    entries = deviation * jax.random.normal(key, dims, jnp.float32)
    if cuts:
        entries = entries * block_levels(key, dims, cuts, -0.22, 0.18)
    return jnp.clip(entries, -bound, bound).astype(held_as)


def setup_inputs(seed: int = 0, part: int = 0) -> dict:
    splits = jax.random.split(jax.random.key(seed), 16)
    part_keys = jax.random.split(jax.random.fold_in(splits[15], part), 16)
    hidden = bell_draw(part_keys[0], (STEPS, BEAM_ROWS, D), 1.0, 6.0, ((1, 16),))
    norm_gain = jnp.clip(1.0 + 0.1 * jax.random.normal(splits[1], (D,), jnp.float32), 0.5, 1.5)
    q_weight = bell_draw(splits[2], (D, QW), D ** -0.5, 0.0625, ((1, 16),))
    q_bias = bell_draw(splits[3], (QW,), 0.5, 3.0, ((0, 16),), jnp.float32)
    kv_weight = bell_draw(splits[4], (D, 2, KVW), D ** -0.5, 0.0625, ((2, 16),))
    kv_bias = bell_draw(splits[5], (2, KVW), 1.0, 5.0, ((1, 16),), jnp.float32)
    o_weight = bell_draw(splits[6], (QW, D), QW ** -0.5, 0.0625, ((1, 16),))
    prefix_key_cache = draw_prefix_key_cache(jax.random.fold_in(jax.random.fold_in(splits[15], part), 71), part)
    prefix_value_cache = bell_draw(part_keys[8], (NPREF, PREFIX_LENGTH, KVW), 2.0, 12.0, ((1, 16),))
    prefix_index = draw_prefix_index(jax.random.fold_in(jax.random.fold_in(splits[15], part), 71), part)
    prefix_lens = draw_prefix_lens(jax.random.fold_in(jax.random.fold_in(splits[15], part), 71), part)
    tail_key_cache = bell_draw(part_keys[11], (BEAM_ROWS, TAIL_LENGTH, KVW), 2.0, 12.0, ((0, 16),))
    tail_value_cache = bell_draw(part_keys[12], (BEAM_ROWS, TAIL_LENGTH, KVW), 2.0, 12.0, ((0, 16),))
    tail_lens = draw_tail_lens(jax.random.fold_in(jax.random.fold_in(splits[15], part), 71), part)
    parents = draw_parents(jax.random.fold_in(jax.random.fold_in(splits[15], part), 71), part)
    return dict(hidden=hidden, norm_gain=norm_gain, q_weight=q_weight, q_bias=q_bias, kv_weight=kv_weight, kv_bias=kv_bias, o_weight=o_weight, prefix_key_cache=prefix_key_cache, prefix_value_cache=prefix_value_cache, prefix_index=prefix_index, prefix_lens=prefix_lens, tail_key_cache=tail_key_cache, tail_value_cache=tail_value_cache, tail_lens=tail_lens, parents=parents)


EPS = 1e-06
NEG = -1e+30
ROPE_BASE = 1000000.0

def rope_parts(positions, head_size):
    half = head_size // 2
    freqs = np.power(ROPE_BASE, -np.arange(half) * 2.0 / head_size)
    angle = positions.astype(jnp.float32)[:, None] * jnp.asarray(freqs, jnp.float32)[None, :]
    return (jnp.cos(angle), jnp.sin(angle))

def apply_rotation(value_rows, cosine_table, sine_table):
    half = value_rows.shape[-1] // 2
    first = value_rows[..., :half]
    second = value_rows[..., half:]
    cosine_table = cosine_table[:, None, :]
    sine_table = sine_table[:, None, :]
    return jnp.concatenate([first * cosine_table - second * sine_table, second * cosine_table + first * sine_table], axis=-1)

def reference(hidden, norm_gain, q_weight, q_bias, kv_weight, kv_bias, o_weight, prefix_key_cache, prefix_value_cache, prefix_index, prefix_lens, tail_key_cache, tail_value_cache, tail_lens, parents):
    head_groups = PREFIX_LENGTH // PREFIX_PER_CHIP
    score_scale = 1.0 / math.sqrt(HEAD_DIM)
    row_ids = jnp.arange(BEAM_ROWS, dtype=jnp.int32)
    prompt_of = row_ids // BEAM_COUNT
    ancestors = row_ids
    makers = []
    fresh_keys = []
    current_values = []
    results = []
    kv_matrix = kv_weight.reshape(D, 2 * KVW)
    kv_shift = kv_bias.reshape(2 * KVW)
    group_ids = jnp.arange(head_groups, dtype=jnp.int32)
    for step in range(STEPS):
        chosen = parents[step]
        ancestors = ancestors[chosen]
        makers = [item[chosen] for item in makers] + [row_ids]
        inputs = hidden[step].astype(jnp.float32)
        normed = (inputs * lax.rsqrt(lax.optimization_barrier(jnp.mean(inputs * inputs, axis=-1, keepdims=True)) + EPS) * norm_gain).astype(jnp.bfloat16)
        queries = (jnp.dot(normed, q_weight, preferred_element_type=jnp.float32) + q_bias).astype(jnp.bfloat16)
        current_key_value = (jnp.dot(normed, kv_matrix, preferred_element_type=jnp.float32) + kv_shift).astype(jnp.bfloat16).reshape(BEAM_ROWS, 2, KVW)
        positions = prefix_lens[prompt_of] + tail_lens[ancestors] + step
        cosine_table, sine_table = rope_parts(positions, HEAD_DIM)
        rotated_rows = apply_rotation(queries.astype(jnp.float32).reshape(BEAM_ROWS, QUERY_HEADS, HEAD_DIM), cosine_table, sine_table).astype(jnp.bfloat16)
        current_keys = apply_rotation(current_key_value[:, 0].astype(jnp.float32).reshape(BEAM_ROWS, KEY_HEADS, HEAD_DIM), cosine_table, sine_table).astype(jnp.bfloat16)
        fresh_keys.append(current_keys)
        current_values.append(current_key_value[:, 1].reshape(BEAM_ROWS, KEY_HEADS, HEAD_DIM))
        key_stack = jnp.stack(fresh_keys, 0)
        value_stack = jnp.stack(current_values, 0)
        lineage = jnp.stack(makers, 1)
        decode_depth = step + 1

        def attend(prompt):
            start_offset = prompt * BEAM_COUNT
            query_rows = lax.dynamic_slice_in_dim(rotated_rows, start_offset, BEAM_COUNT, 0).astype(jnp.float32).reshape(BEAM_COUNT, KEY_HEADS, GROUP_SIZE, HEAD_DIM)
            entry_point = prefix_index[prompt]
            length = prefix_lens[prompt]
            key_rows = lax.dynamic_index_in_dim(prefix_key_cache, entry_point, 0, keepdims=False).astype(jnp.float32).reshape(PREFIX_LENGTH, KEY_HEADS, HEAD_DIM)
            value_rows = lax.dynamic_index_in_dim(prefix_value_cache, entry_point, 0, keepdims=False).astype(jnp.float32).reshape(head_groups, PREFIX_PER_CHIP, KEY_HEADS, HEAD_DIM)
            valid = (jnp.arange(PREFIX_LENGTH, dtype=jnp.int32) < length).reshape(head_groups, PREFIX_PER_CHIP)
            score_matrix = jnp.einsum('cixw,eiw->cixe', query_rows, key_rows).reshape(BEAM_COUNT, KEY_HEADS, GROUP_SIZE, head_groups, PREFIX_PER_CHIP) * score_scale
            score_matrix = jnp.where(valid, score_matrix, NEG)
            owner_rows = lax.dynamic_slice_in_dim(ancestors, start_offset, BEAM_COUNT, 0)
            tail_key_rows = tail_key_cache[owner_rows].astype(jnp.float32).reshape(BEAM_COUNT, TAIL_LENGTH, KEY_HEADS, HEAD_DIM)
            tail_value_rows = tail_value_cache[owner_rows].astype(jnp.float32).reshape(BEAM_COUNT, TAIL_LENGTH, KEY_HEADS, HEAD_DIM)
            tail_ok = jnp.arange(TAIL_LENGTH, dtype=jnp.int32)[None, :] < tail_lens[owner_rows][:, None]
            tail_scores = jnp.einsum('bkgd,btkd->bkgt', query_rows, tail_key_rows) * score_scale
            tail_scores = jnp.where(tail_ok[:, None, None, :], tail_scores, NEG)
            tail_head_group = owner_rows // ROW_DEV
            tail_hot = tail_head_group[:, None] == group_ids[None, :]
            made = lax.dynamic_slice_in_dim(lineage, start_offset, BEAM_COUNT, 0)
            made_k = key_stack[jnp.arange(decode_depth, dtype=jnp.int32)[None, :], made].astype(jnp.float32)
            made_v = value_stack[jnp.arange(decode_depth, dtype=jnp.int32)[None, :], made].astype(jnp.float32)
            made_scores = jnp.einsum('bkgd,bjkd->bkgj', query_rows, made_k) * score_scale
            produced_group = made // ROW_DEV
            made_hot = produced_group[:, :, None] == group_ids[None, None, :]
            group_maximum = jnp.maximum(score_matrix.max(-1), jnp.where(tail_hot[:, None, None, :], tail_scores.max(-1)[..., None], NEG))
            group_maximum = jnp.maximum(group_maximum, jnp.where(made_hot[:, None, None, :, :], made_scores[..., None], NEG).max(3))
            weights = jnp.where(valid, jnp.exp(score_matrix - group_maximum[..., None]), 0.0)
            total = weights.sum(-1)
            numer = jnp.einsum('bkgns,nskd->bkgnd', weights.astype(jnp.bfloat16).astype(jnp.float32), value_rows)
            tail_maximum = jnp.take_along_axis(group_maximum, jnp.broadcast_to(tail_head_group[:, None, None, None], (BEAM_COUNT, KEY_HEADS, GROUP_SIZE, 1)), axis=3)
            tail_w = jnp.where(tail_ok[:, None, None, :], jnp.exp(tail_scores - tail_maximum), 0.0)
            tail_hot_f = tail_hot.astype(jnp.float32)
            total = total + tail_hot_f[:, None, None, :] * tail_w.sum(-1)[..., None]
            tail_num = jnp.einsum('bkgt,btkd->bkgd', tail_w.astype(jnp.bfloat16).astype(jnp.float32), tail_value_rows)
            numer = numer + tail_hot_f[:, None, None, :, None] * tail_num[:, :, :, None, :]
            produced_top = jnp.take_along_axis(group_maximum, jnp.broadcast_to(produced_group[:, None, None, :], (BEAM_COUNT, KEY_HEADS, GROUP_SIZE, decode_depth)), axis=3)
            made_w = jnp.exp(made_scores - produced_top)
            made_hot_f = made_hot.astype(jnp.float32)
            total = total + jnp.einsum('bkgj,bjn->bkgn', made_w, made_hot_f)
            numer = numer + jnp.einsum('bkgj,bjn,bjkd->bkgnd', made_w.astype(jnp.bfloat16).astype(jnp.float32), made_hot_f, made_v)
            rounded = lax.optimization_barrier(numer.astype(jnp.bfloat16))
            numer = rounded.astype(jnp.float32)
            top = group_maximum.max(-1)
            scaled = jnp.exp(group_maximum - top[..., None])
            denom = (scaled * total).sum(-1)
            result = jnp.einsum('bkgn,bkgnd->bkgd', scaled, numer) / denom[..., None]
            return result.reshape(BEAM_COUNT, QW).astype(jnp.bfloat16)
        attention = lax.map(attend, jnp.arange(PROMPTS, dtype=jnp.int32)).reshape(BEAM_ROWS, QW)
        results.append(jnp.dot(attention, o_weight, preferred_element_type=jnp.float32).astype(jnp.bfloat16))
    return jnp.stack(results, 0)
```

```python
import math

import jax
import jax.numpy as jnp
import numpy as np
from jax import lax
from jax.sharding import PartitionSpec as P

QUERY_HEADS = 64
KEY_HEADS = 8
HEAD_DIM = 128
BEAM_COUNT = 16
STEPS = 3


EPS = 1e-06
NEG = -1e30
ROPE_BASE = 1000000.0


def rope_parts(positions, head_size):
    half = head_size // 2
    freqs = np.power(ROPE_BASE, -np.arange(half) * 2.0 / head_size)
    angle = positions.astype(jnp.float32)[:, None] * jnp.asarray(freqs, jnp.float32)[None, :]
    return (jnp.cos(angle), jnp.sin(angle))


def apply_rotation(value_rows, cosine_table, sine_table):
    half = value_rows.shape[-1] // 2
    first = value_rows[..., :half]
    second = value_rows[..., half:]
    cosine_table = cosine_table[:, None, :]
    sine_table = sine_table[:, None, :]
    return jnp.concatenate(
        [first * cosine_table - second * sine_table, second * cosine_table + first * sine_table],
        axis=-1,
    )


def local_by_rows(
    hidden,
    norm_gain,
    q_weight,
    q_bias,
    kv_weight,
    kv_bias,
    o_weight,
    prefix_key_cache,
    prefix_value_cache,
    prefix_index,
    prefix_lens,
    tail_key_cache,
    tail_value_cache,
    tail_lens,
    parents,
):
    devices = lax.axis_size("beam")
    me = lax.axis_index("beam")
    rows_per_chip = hidden.shape[1]
    width = hidden.shape[2]
    all_rows = rows_per_chip * devices
    prompt_batch = all_rows // BEAM_COUNT
    head_group = QUERY_HEADS // KEY_HEADS
    q_width = QUERY_HEADS * HEAD_DIM
    q_cols = q_weight.shape[1]
    kv_cols = kv_weight.shape[2]
    prefix_slice = prefix_key_cache.shape[1]
    tail_cache = tail_key_cache.shape[1]
    score_scale = 1.0 / math.sqrt(HEAD_DIM)
    row_ids = jnp.arange(all_rows, dtype=jnp.int32)
    prompt_of = row_ids // BEAM_COUNT
    first_row = me * rows_per_chip
    my_prompt = first_row // BEAM_COUNT
    slot_ids = first_row + jnp.arange(rows_per_chip, dtype=jnp.int32)
    mine = (jnp.arange(prompt_batch, dtype=jnp.int32) == my_prompt)[:, None, None, None]
    joint = jnp.concatenate([q_weight, kv_weight.reshape(width, 2 * kv_cols)], axis=1)
    joint_bias = jnp.concatenate([q_bias, kv_bias.reshape(2 * kv_cols)])
    slice_keys = jnp.take(prefix_key_cache, prefix_index, axis=0).reshape(
        prompt_batch, prefix_slice, KEY_HEADS, HEAD_DIM
    )
    slice_values = jnp.take(prefix_value_cache, prefix_index, axis=0).reshape(
        prompt_batch, prefix_slice, KEY_HEADS, HEAD_DIM
    )
    slab_ok = (me * prefix_slice + jnp.arange(prefix_slice, dtype=jnp.int32))[
        None, :
    ] < prefix_lens[:, None]
    slab_ok = slab_ok[:, None, None, None, :]
    tail_key_rows = tail_key_cache.reshape(rows_per_chip, tail_cache, KEY_HEADS, HEAD_DIM)
    tail_value_rows = tail_value_cache.reshape(rows_per_chip, tail_cache, KEY_HEADS, HEAD_DIM)
    own_lens = lax.dynamic_slice_in_dim(tail_lens, first_row, rows_per_chip, 0)
    tail_ok = jnp.arange(tail_cache, dtype=jnp.int32)[None, :] < own_lens[:, None]
    ancestors = row_ids
    makers = []
    fresh_keys = []
    current_values = []
    results = []
    for step in range(STEPS):
        chosen = parents[step]
        ancestors = ancestors[chosen]
        makers = [item[chosen] for item in makers] + [row_ids]
        value_rows = lax.all_gather(hidden[step], "beam", axis=0, tiled=True).astype(jnp.float32)
        normed = (
            value_rows
            * lax.rsqrt(jnp.mean(value_rows * value_rows, axis=-1, keepdims=True) + EPS)
            * norm_gain
        ).astype(jnp.bfloat16)
        projected = jnp.dot(normed, joint, preferred_element_type=jnp.float32) + joint_bias
        q_part = projected[:, :q_cols].astype(jnp.bfloat16)
        kv_part = projected[:, q_cols:].astype(jnp.bfloat16).reshape(all_rows, 2, kv_cols)
        positions = prefix_lens[prompt_of] + tail_lens[ancestors] + step
        cosine_table, sine_table = rope_parts(positions, HEAD_DIM)
        q_full, kv_full = (
            lax.all_gather(q_part[:, None, :], "beam", axis=2, tiled=True),
            lax.all_gather(kv_part, "beam", axis=2, tiled=True),
        )
        q_all = q_full[:, 0, :]
        owned_key_value = lax.dynamic_slice_in_dim(kv_full, first_row, rows_per_chip, 0)
        rotated_rows = apply_rotation(
            q_all.astype(jnp.float32).reshape(all_rows, QUERY_HEADS, HEAD_DIM),
            cosine_table,
            sine_table,
        ).astype(jnp.bfloat16)
        local_cosine = lax.dynamic_slice_in_dim(cosine_table, first_row, rows_per_chip, 0)
        local_sine = lax.dynamic_slice_in_dim(sine_table, first_row, rows_per_chip, 0)
        new_key = apply_rotation(
            owned_key_value[:, 0].astype(jnp.float32).reshape(rows_per_chip, KEY_HEADS, HEAD_DIM),
            local_cosine,
            local_sine,
        ).astype(jnp.bfloat16)
        fresh_keys.append(new_key)
        current_values.append(owned_key_value[:, 1].reshape(rows_per_chip, KEY_HEADS, HEAD_DIM))
        query_rows = rotated_rows.reshape(prompt_batch, BEAM_COUNT, KEY_HEADS, head_group, HEAD_DIM)
        pre_scores = (
            jnp.einsum(
                "pbkgd,pskd->pbkgs", query_rows, slice_keys, preferred_element_type=jnp.float32
            )
            * score_scale
        )
        pre_scores = jnp.where(slab_ok, pre_scores, NEG)
        local_q = lax.dynamic_index_in_dim(query_rows, my_prompt, 0, keepdims=False)
        local_anc = lax.dynamic_slice_in_dim(ancestors, my_prompt * BEAM_COUNT, BEAM_COUNT, 0)
        t_scores = (
            jnp.einsum(
                "bkgd,itkd->bkgit", local_q, tail_key_rows, preferred_element_type=jnp.float32
            )
            * score_scale
        )
        t_valid = (local_anc[:, None] == slot_ids[None, :])[:, None, None, :, None] & tail_ok[
            None, None, None, :, :
        ]
        t_scores = jnp.where(t_valid, t_scores, NEG)
        f_keys = jnp.stack(fresh_keys, 0)
        f_values = jnp.stack(current_values, 0)
        local_made = jnp.stack(
            [
                lax.dynamic_slice_in_dim(item, my_prompt * BEAM_COUNT, BEAM_COUNT, 0)
                for item in makers
            ],
            1,
        )
        f_valid = (local_made[:, :, None] == slot_ids[None, None, :])[:, None, None, :, :]
        f_scores = (
            jnp.einsum("bkgd,jikd->bkgji", local_q, f_keys, preferred_element_type=jnp.float32)
            * score_scale
        )
        f_scores = jnp.where(f_valid, f_scores, NEG)
        local_max = jnp.maximum(t_scores.max(axis=(3, 4)), f_scores.max(axis=(3, 4)))
        pre_max = pre_scores.max(-1)
        group_maximum = jnp.where(mine, jnp.maximum(pre_max, local_max[None]), pre_max)
        mine_max = lax.dynamic_index_in_dim(group_maximum, my_prompt, 0, keepdims=False)
        pre_w = jnp.where(slab_ok, jnp.exp(pre_scores - group_maximum[..., None]), 0.0)
        totals = pre_w.sum(-1)
        numer = jnp.einsum(
            "pbkgs,pskd->pbkgd",
            pre_w.astype(jnp.bfloat16),
            slice_values,
            preferred_element_type=jnp.float32,
        )
        t_w = jnp.where(t_valid, jnp.exp(t_scores - mine_max[..., None, None]), 0.0)
        f_w = jnp.where(f_valid, jnp.exp(f_scores - mine_max[..., None, None]), 0.0)
        local_total = t_w.sum(axis=(3, 4)) + f_w.sum(axis=(3, 4))
        local_num = jnp.einsum(
            "bkgit,itkd->bkgd",
            t_w.astype(jnp.bfloat16),
            tail_value_rows,
            preferred_element_type=jnp.float32,
        )
        local_num = local_num + jnp.einsum(
            "bkgji,jikd->bkgd",
            f_w.astype(jnp.bfloat16),
            f_values,
            preferred_element_type=jnp.float32,
        )
        totals = jnp.where(mine, totals + local_total[None], totals)
        numer = jnp.where(mine[..., None], numer + local_num[None], numer)
        sending = numer.astype(jnp.bfloat16).reshape(devices, rows_per_chip, q_width)
        parts = lax.all_to_all(sending, "beam", split_axis=0, concat_axis=0, tiled=True)
        maxima, sums = (
            lax.all_to_all(
                group_maximum.reshape(devices, rows_per_chip, QUERY_HEADS),
                "beam",
                split_axis=0,
                concat_axis=0,
                tiled=True,
            ),
            lax.all_to_all(
                totals.reshape(devices, rows_per_chip, QUERY_HEADS),
                "beam",
                split_axis=0,
                concat_axis=0,
                tiled=True,
            ),
        )
        top = maxima.max(0)
        factors = jnp.exp(maxima - top[None])
        denom = (factors * sums).sum(0)
        combined = jnp.einsum(
            "srh,srhd->rhd",
            factors,
            parts.reshape(devices, rows_per_chip, QUERY_HEADS, HEAD_DIM),
            preferred_element_type=jnp.float32,
        )
        attention = (
            (combined / denom[..., None]).reshape(rows_per_chip, q_width).astype(jnp.bfloat16)
        )
        out_cols = jnp.dot(
            lax.all_gather(attention, "beam", axis=0, tiled=True),
            o_weight,
            preferred_element_type=jnp.float32,
        )
        results.append(out_cols.astype(jnp.bfloat16))
    return jnp.stack(results, 0)


def lineage_tables(parents, prefix_lens, tail_lens, rows_per_chip, devices):
    all_rows = parents.shape[1]
    row_ids = jnp.arange(all_rows, dtype=jnp.int32)
    ancestors = row_ids
    makers = []
    anc_steps, pos_steps, maker_steps = [], [], []
    base = prefix_lens[row_ids // BEAM_COUNT]
    for step in range(STEPS):
        hot = parents[step][:, None] == row_ids[None, :]
        pick = lambda item: jnp.sum(jnp.where(hot, item[None, :], 0), axis=1)
        ancestors = pick(ancestors)
        makers = [pick(item) for item in makers] + [row_ids]
        lens = jnp.sum(jnp.where(ancestors[:, None] == row_ids[None, :], tail_lens[None, :], 0), axis=1)
        anc_steps.append(ancestors)
        pos_steps.append(base + lens + step)
        maker_steps.append(jnp.stack(makers + [jnp.full_like(row_ids, -1)] * (STEPS - 1 - step), 0))

    def order(table):
        lead = table.shape[1:-1]
        table = table.reshape((STEPS,) + lead + (devices, rows_per_chip))
        table = jnp.moveaxis(table, -2, 0)
        table = jnp.moveaxis(table, 1, -2)
        return jnp.moveaxis(table, 0, -3).reshape(lead + (STEPS * all_rows,))

    return order(jnp.stack(anc_steps, 0)), order(jnp.stack(pos_steps, 0)), order(jnp.stack(maker_steps, 0))


def local(
    hidden,
    norm_gain,
    q_weight,
    q_bias,
    kv_weight,
    kv_bias,
    o_weight,
    prefix_key_cache,
    prefix_value_cache,
    prefix_index,
    prefix_lens,
    tail_key_cache,
    tail_value_cache,
    tail_lens,
    parents,
):
    devices = lax.axis_size("beam")
    me = lax.axis_index("beam")
    rpc = hidden.shape[1]
    width = hidden.shape[2]
    if QUERY_HEADS % devices or 2 * kv_weight.shape[2] != HEAD_DIM:
        return local_by_rows(
            hidden, norm_gain, q_weight, q_bias, kv_weight, kv_bias, o_weight, prefix_key_cache,
            prefix_value_cache, prefix_index, prefix_lens, tail_key_cache, tail_value_cache, tail_lens, parents,
        )
    own = STEPS * rpc
    rows = own * devices
    prompts = prefix_index.shape[0]
    ppr = rows // prompts
    heads = QUERY_HEADS // devices
    group = QUERY_HEADS // KEY_HEADS
    q_cols = q_weight.shape[1]
    kv_cols = kv_weight.shape[2]
    slab = prefix_key_cache.shape[1]
    tail = tail_key_cache.shape[1]
    score_scale = 1.0 / math.sqrt(HEAD_DIM)
    my_prompt = me * rpc // BEAM_COUNT
    anc, pos, made = lineage_tables(parents, prefix_lens, tail_lens, rpc, devices)

    x = hidden.astype(jnp.float32)
    normed = (x * lax.rsqrt(jnp.mean(x * x, axis=-1, keepdims=True) + EPS) * norm_gain).astype(jnp.bfloat16)
    normed = lax.all_gather(normed.reshape(own, width), "beam", axis=0, tiled=True)
    q = (jnp.dot(normed, q_weight, preferred_element_type=jnp.float32) + q_bias).astype(jnp.bfloat16)
    kv = jnp.dot(normed, kv_weight.reshape(width, 2 * kv_cols), preferred_element_type=jnp.float32)
    kv = (kv + kv_bias.reshape(2 * kv_cols)).astype(jnp.bfloat16)
    cosine, sine = rope_parts(pos, HEAD_DIM)
    cosine2 = jnp.concatenate([cosine, cosine], 1)
    sine2 = jnp.concatenate([-sine, sine], 1)

    def rotate(v):
        v = v.astype(jnp.float32)
        return (v * cosine2 + jnp.roll(v, HEAD_DIM // 2, axis=-1) * sine2).astype(jnp.bfloat16)

    pieces = [rotate(q[:, h * HEAD_DIM : (h + 1) * HEAD_DIM]) for h in range(heads)] + [kv]
    full = lax.all_gather(jnp.stack(pieces, 0), "beam", axis=0)
    query = full[:, :heads].reshape(KEY_HEADS, group, prompts, ppr, HEAD_DIM)
    mine6 = lax.dynamic_slice_in_dim(full[:, heads], me * own, own, 1).reshape(devices, own, 2, kv_cols)
    mine6 = jnp.transpose(mine6, (2, 1, 0, 3)).reshape(2, own, KEY_HEADS, HEAD_DIM)
    my_cos = lax.dynamic_slice_in_dim(cosine2, me * own, own, 0)[:, None]
    my_sin = lax.dynamic_slice_in_dim(sine2, me * own, own, 0)[:, None]
    fk = mine6[0].astype(jnp.float32)
    fk = (fk * my_cos + jnp.roll(fk, HEAD_DIM // 2, axis=-1) * my_sin).astype(jnp.bfloat16)
    fv = mine6[1]

    num, gmax, gsum = attend(
        query, fk, fv, prefix_key_cache, prefix_value_cache, prefix_index, prefix_lens,
        tail_key_cache, tail_value_cache, tail_lens, anc, made, me, my_prompt, rpc, score_scale,
    )
    parts = lax.all_to_all(num.reshape(devices, heads * rows, HEAD_DIM), "beam", 0, 0, tiled=True)
    stats = jnp.stack([gmax.reshape(devices, heads, rows), gsum.reshape(devices, heads, rows)], 1)
    stats = lax.all_to_all(stats, "beam", 0, 0, tiled=True)
    maxima, sums = stats[:, 0], stats[:, 1]
    factors = jnp.exp(maxima - maxima.max(0)[None])
    denom = (factors * sums).sum(0)
    parts = parts.reshape(devices, heads, rows, HEAD_DIM).astype(jnp.float32)
    att = (factors[..., None] * parts).sum(0) / denom[..., None]
    att = jnp.transpose(att.astype(jnp.bfloat16), (1, 0, 2)).reshape(rows, heads * HEAD_DIM)
    att = lax.all_gather(att, "beam", axis=1, tiled=True)
    out = jnp.dot(att, o_weight, preferred_element_type=jnp.float32).astype(jnp.bfloat16)
    out = out.reshape(devices, STEPS, rpc, out.shape[1])
    return jnp.transpose(out, (1, 0, 2, 3)).reshape(STEPS, devices * rpc, out.shape[3])


def attend(
    query, fk, fv, prefix_keys, prefix_values, prefix_index, prefix_lens,
    tail_keys, tail_values, tail_lens, anc, made, me, my_prompt, rpc, score_scale,
):
    khs, group, prompts, ppr, hd = query.shape
    slab = prefix_keys.shape[1]
    tail = tail_keys.shape[1]
    own = fk.shape[0]
    rows = prompts * ppr
    first = me * rpc
    pk = jnp.take(prefix_keys, prefix_index, axis=0).reshape(prompts, slab, khs, hd)
    pv = jnp.take(prefix_values, prefix_index, axis=0).reshape(prompts, slab, khs, hd)
    s = jnp.einsum("kgpbd,pskd->kpgbs", query, pk, preferred_element_type=jnp.float32) * score_scale
    ok = (me * slab + jnp.arange(slab, dtype=jnp.int32))[None, :] < prefix_lens[:, None]
    ok = ok[None, :, None, None, :]
    s = jnp.where(ok, s, NEG)
    lq = lax.dynamic_index_in_dim(query, my_prompt, 2, keepdims=False).reshape(khs, group, ppr, hd)
    lanc = lax.dynamic_slice_in_dim(anc, my_prompt * ppr, ppr, 0)
    lmade = lax.dynamic_slice_in_dim(made, my_prompt * ppr, ppr, 1)
    own_lens = lax.dynamic_slice_in_dim(tail_lens, first, rpc, 0)
    slot = first + jnp.arange(rpc, dtype=jnp.int32)
    t_ok = (lanc[:, None] == slot[None, :])[:, :, None] & (
        jnp.arange(tail, dtype=jnp.int32)[None, None, :] < own_lens[None, :, None]
    )
    f_ok = lmade.T[:, :, None] == slot[None, None, :]
    l_ok = jnp.concatenate([t_ok.reshape(ppr, rpc * tail), f_ok.reshape(ppr, own)], 1)[None, None]
    lk = jnp.concatenate([tail_keys.reshape(rpc * tail, khs, hd), fk], 0)
    lv = jnp.concatenate([tail_values.reshape(rpc * tail, khs, hd), fv], 0)
    ls = jnp.einsum("kgbd,tkd->kgbt", lq, lk, preferred_element_type=jnp.float32) * score_scale
    ls = jnp.where(l_ok, ls, NEG)
    mine = (jnp.arange(prompts, dtype=jnp.int32) == my_prompt)[None, :, None, None]
    gmax = jnp.maximum(s.max(-1), jnp.where(mine, ls.max(-1)[:, None], NEG))
    lmax = lax.dynamic_index_in_dim(gmax, my_prompt, 1, keepdims=False)
    w = jnp.where(ok, jnp.exp(s - gmax[..., None]), 0.0)
    lw = jnp.where(l_ok, jnp.exp(ls - lmax[..., None]), 0.0)
    gsum = w.sum(-1) + jnp.where(mine, lw.sum(-1)[:, None], 0.0)
    num = jnp.einsum("kpgbs,pskd->kpgbd", w.astype(jnp.bfloat16), pv, preferred_element_type=jnp.float32)
    lnum = jnp.einsum("kgbt,tkd->kgbd", lw.astype(jnp.bfloat16), lv, preferred_element_type=jnp.float32)
    num = num + jnp.where(mine[..., None], lnum[:, None], 0.0)
    num = jnp.swapaxes(num.astype(jnp.bfloat16), 1, 2).reshape(khs * group, rows, hd)
    return num, jnp.swapaxes(gmax, 1, 2).reshape(khs * group, rows), jnp.swapaxes(gsum, 1, 2).reshape(khs * group, rows)


def solution(mesh):
    return jax.shard_map(
        local,
        mesh=mesh,
        in_specs=(
            P(None, ("grp", "beam"), None),
            P(),
            P(None, "beam"),
            P("beam"),
            P(None, None, "beam"),
            P(None, "beam"),
            P(None, "beam"),
            P("grp", "beam", None),
            P("grp", "beam", None),
            P("grp"),
            P("grp"),
            P(("grp", "beam"), None, None),
            P(("grp", "beam"), None, None),
            P("grp"),
            P(None, "grp"),
        ),
        out_specs=P(None, "grp", "beam"),
        check_vma=False,
    )
```

```python
import math

import jax
import jax.numpy as jnp
import numpy as np
from jax import lax
from jax.experimental import pallas as pl
from jax.experimental.pallas import tpu as pltpu
from jax.sharding import PartitionSpec as P

QUERY_HEADS = 64
KEY_HEADS = 8
HEAD_DIM = 128
BEAM_COUNT = 16
STEPS = 3


EPS = 1e-06
NEG = -1e30
ROPE_BASE = 1000000.0


def rope_parts(positions, head_size):
    half = head_size // 2
    freqs = np.power(ROPE_BASE, -np.arange(half) * 2.0 / head_size)
    angle = positions.astype(jnp.float32)[:, None] * jnp.asarray(freqs, jnp.float32)[None, :]
    return (jnp.cos(angle), jnp.sin(angle))


def apply_rotation(value_rows, cosine_table, sine_table):
    half = value_rows.shape[-1] // 2
    first = value_rows[..., :half]
    second = value_rows[..., half:]
    cosine_table = cosine_table[:, None, :]
    sine_table = sine_table[:, None, :]
    return jnp.concatenate(
        [first * cosine_table - second * sine_table, second * cosine_table + first * sine_table],
        axis=-1,
    )


def local_by_rows(
    hidden,
    norm_gain,
    q_weight,
    q_bias,
    kv_weight,
    kv_bias,
    o_weight,
    prefix_key_cache,
    prefix_value_cache,
    prefix_index,
    prefix_lens,
    tail_key_cache,
    tail_value_cache,
    tail_lens,
    parents,
):
    devices = lax.axis_size("beam")
    me = lax.axis_index("beam")
    rows_per_chip = hidden.shape[1]
    width = hidden.shape[2]
    all_rows = rows_per_chip * devices
    prompt_batch = all_rows // BEAM_COUNT
    head_group = QUERY_HEADS // KEY_HEADS
    q_width = QUERY_HEADS * HEAD_DIM
    q_cols = q_weight.shape[1]
    kv_cols = kv_weight.shape[2]
    prefix_slice = prefix_key_cache.shape[1]
    tail_cache = tail_key_cache.shape[1]
    score_scale = 1.0 / math.sqrt(HEAD_DIM)
    row_ids = jnp.arange(all_rows, dtype=jnp.int32)
    prompt_of = row_ids // BEAM_COUNT
    first_row = me * rows_per_chip
    my_prompt = first_row // BEAM_COUNT
    slot_ids = first_row + jnp.arange(rows_per_chip, dtype=jnp.int32)
    mine = (jnp.arange(prompt_batch, dtype=jnp.int32) == my_prompt)[:, None, None, None]
    joint = jnp.concatenate([q_weight, kv_weight.reshape(width, 2 * kv_cols)], axis=1)
    joint_bias = jnp.concatenate([q_bias, kv_bias.reshape(2 * kv_cols)])
    slice_keys = jnp.take(prefix_key_cache, prefix_index, axis=0).reshape(
        prompt_batch, prefix_slice, KEY_HEADS, HEAD_DIM
    )
    slice_values = jnp.take(prefix_value_cache, prefix_index, axis=0).reshape(
        prompt_batch, prefix_slice, KEY_HEADS, HEAD_DIM
    )
    slab_ok = (me * prefix_slice + jnp.arange(prefix_slice, dtype=jnp.int32))[
        None, :
    ] < prefix_lens[:, None]
    slab_ok = slab_ok[:, None, None, None, :]
    tail_key_rows = tail_key_cache.reshape(rows_per_chip, tail_cache, KEY_HEADS, HEAD_DIM)
    tail_value_rows = tail_value_cache.reshape(rows_per_chip, tail_cache, KEY_HEADS, HEAD_DIM)
    own_lens = lax.dynamic_slice_in_dim(tail_lens, first_row, rows_per_chip, 0)
    tail_ok = jnp.arange(tail_cache, dtype=jnp.int32)[None, :] < own_lens[:, None]
    ancestors = row_ids
    makers = []
    fresh_keys = []
    current_values = []
    results = []
    for step in range(STEPS):
        chosen = parents[step]
        ancestors = ancestors[chosen]
        makers = [item[chosen] for item in makers] + [row_ids]
        value_rows = lax.all_gather(hidden[step], "beam", axis=0, tiled=True).astype(jnp.float32)
        normed = (
            value_rows
            * lax.rsqrt(jnp.mean(value_rows * value_rows, axis=-1, keepdims=True) + EPS)
            * norm_gain
        ).astype(jnp.bfloat16)
        projected = jnp.dot(normed, joint, preferred_element_type=jnp.float32) + joint_bias
        q_part = projected[:, :q_cols].astype(jnp.bfloat16)
        kv_part = projected[:, q_cols:].astype(jnp.bfloat16).reshape(all_rows, 2, kv_cols)
        positions = prefix_lens[prompt_of] + tail_lens[ancestors] + step
        cosine_table, sine_table = rope_parts(positions, HEAD_DIM)
        q_full, kv_full = (
            lax.all_gather(q_part[:, None, :], "beam", axis=2, tiled=True),
            lax.all_gather(kv_part, "beam", axis=2, tiled=True),
        )
        q_all = q_full[:, 0, :]
        owned_key_value = lax.dynamic_slice_in_dim(kv_full, first_row, rows_per_chip, 0)
        rotated_rows = apply_rotation(
            q_all.astype(jnp.float32).reshape(all_rows, QUERY_HEADS, HEAD_DIM),
            cosine_table,
            sine_table,
        ).astype(jnp.bfloat16)
        local_cosine = lax.dynamic_slice_in_dim(cosine_table, first_row, rows_per_chip, 0)
        local_sine = lax.dynamic_slice_in_dim(sine_table, first_row, rows_per_chip, 0)
        new_key = apply_rotation(
            owned_key_value[:, 0].astype(jnp.float32).reshape(rows_per_chip, KEY_HEADS, HEAD_DIM),
            local_cosine,
            local_sine,
        ).astype(jnp.bfloat16)
        fresh_keys.append(new_key)
        current_values.append(owned_key_value[:, 1].reshape(rows_per_chip, KEY_HEADS, HEAD_DIM))
        query_rows = rotated_rows.reshape(prompt_batch, BEAM_COUNT, KEY_HEADS, head_group, HEAD_DIM)
        pre_scores = (
            jnp.einsum(
                "pbkgd,pskd->pbkgs", query_rows, slice_keys, preferred_element_type=jnp.float32
            )
            * score_scale
        )
        pre_scores = jnp.where(slab_ok, pre_scores, NEG)
        local_q = lax.dynamic_index_in_dim(query_rows, my_prompt, 0, keepdims=False)
        local_anc = lax.dynamic_slice_in_dim(ancestors, my_prompt * BEAM_COUNT, BEAM_COUNT, 0)
        t_scores = (
            jnp.einsum(
                "bkgd,itkd->bkgit", local_q, tail_key_rows, preferred_element_type=jnp.float32
            )
            * score_scale
        )
        t_valid = (local_anc[:, None] == slot_ids[None, :])[:, None, None, :, None] & tail_ok[
            None, None, None, :, :
        ]
        t_scores = jnp.where(t_valid, t_scores, NEG)
        f_keys = jnp.stack(fresh_keys, 0)
        f_values = jnp.stack(current_values, 0)
        local_made = jnp.stack(
            [
                lax.dynamic_slice_in_dim(item, my_prompt * BEAM_COUNT, BEAM_COUNT, 0)
                for item in makers
            ],
            1,
        )
        f_valid = (local_made[:, :, None] == slot_ids[None, None, :])[:, None, None, :, :]
        f_scores = (
            jnp.einsum("bkgd,jikd->bkgji", local_q, f_keys, preferred_element_type=jnp.float32)
            * score_scale
        )
        f_scores = jnp.where(f_valid, f_scores, NEG)
        local_max = jnp.maximum(t_scores.max(axis=(3, 4)), f_scores.max(axis=(3, 4)))
        pre_max = pre_scores.max(-1)
        group_maximum = jnp.where(mine, jnp.maximum(pre_max, local_max[None]), pre_max)
        mine_max = lax.dynamic_index_in_dim(group_maximum, my_prompt, 0, keepdims=False)
        pre_w = jnp.where(slab_ok, jnp.exp(pre_scores - group_maximum[..., None]), 0.0)
        totals = pre_w.sum(-1)
        numer = jnp.einsum(
            "pbkgs,pskd->pbkgd",
            pre_w.astype(jnp.bfloat16),
            slice_values,
            preferred_element_type=jnp.float32,
        )
        t_w = jnp.where(t_valid, jnp.exp(t_scores - mine_max[..., None, None]), 0.0)
        f_w = jnp.where(f_valid, jnp.exp(f_scores - mine_max[..., None, None]), 0.0)
        local_total = t_w.sum(axis=(3, 4)) + f_w.sum(axis=(3, 4))
        local_num = jnp.einsum(
            "bkgit,itkd->bkgd",
            t_w.astype(jnp.bfloat16),
            tail_value_rows,
            preferred_element_type=jnp.float32,
        )
        local_num = local_num + jnp.einsum(
            "bkgji,jikd->bkgd",
            f_w.astype(jnp.bfloat16),
            f_values,
            preferred_element_type=jnp.float32,
        )
        totals = jnp.where(mine, totals + local_total[None], totals)
        numer = jnp.where(mine[..., None], numer + local_num[None], numer)
        sending = numer.astype(jnp.bfloat16).reshape(devices, rows_per_chip, q_width)
        parts = lax.all_to_all(sending, "beam", split_axis=0, concat_axis=0, tiled=True)
        maxima, sums = (
            lax.all_to_all(
                group_maximum.reshape(devices, rows_per_chip, QUERY_HEADS),
                "beam",
                split_axis=0,
                concat_axis=0,
                tiled=True,
            ),
            lax.all_to_all(
                totals.reshape(devices, rows_per_chip, QUERY_HEADS),
                "beam",
                split_axis=0,
                concat_axis=0,
                tiled=True,
            ),
        )
        top = maxima.max(0)
        factors = jnp.exp(maxima - top[None])
        denom = (factors * sums).sum(0)
        combined = jnp.einsum(
            "srh,srhd->rhd",
            factors,
            parts.reshape(devices, rows_per_chip, QUERY_HEADS, HEAD_DIM),
            preferred_element_type=jnp.float32,
        )
        attention = (
            (combined / denom[..., None]).reshape(rows_per_chip, q_width).astype(jnp.bfloat16)
        )
        out_cols = jnp.dot(
            lax.all_gather(attention, "beam", axis=0, tiled=True),
            o_weight,
            preferred_element_type=jnp.float32,
        )
        results.append(out_cols.astype(jnp.bfloat16))
    return jnp.stack(results, 0)


MESH = pl.DeviceIdType.MESH


def place():
    me = lax.axis_index("beam")
    return me, me // 4, me // 2 % 2, me % 2


def at(z, y, c):
    return (z * 2 + y) * 2 + c


def partners(z):
    return [z + 1 - 2 * (z % 2), (z + 2) % 4, 3 - z]


def greet(z, y, c):
    barrier = pltpu.get_barrier_semaphore()
    others = [at(w, y, c) for w in partners(z)] + [at(z, 1 - y, c), at(z, y, 1 - c)]
    for other in others:
        pl.semaphore_signal(barrier, inc=1, device_id={"beam": other}, device_id_type=MESH)
    pl.semaphore_wait(barrier, len(others))


class Gather:
    def __init__(self, x_ref, o_ref, send, recv):
        self.x_ref, self.o_ref, self.send, self.recv = x_ref, o_ref, send, recv
        self.me, self.z, self.y, self.c = place()
        self.sent = []

    def push(self, shard, target, src):
        copy = pltpu.make_async_remote_copy(
            src_ref=src,
            dst_ref=self.o_ref.at[shard],
            send_sem=self.send.at[len(self.sent)],
            recv_sem=self.recv.at[shard],
            device_id={"beam": target},
            device_id_type=MESH,
        )
        copy.start()
        self.sent.append(copy)

    def arrive(self, shard):
        pltpu.make_async_remote_copy(
            src_ref=self.o_ref.at[shard],
            dst_ref=self.o_ref.at[shard],
            send_sem=self.send.at[0],
            recv_sem=self.recv.at[shard],
            device_id={"beam": at(self.z, self.y, 1 - self.c)},
            device_id_type=MESH,
        ).wait_recv()

    def run(self, use):
        z, y, c = self.z, self.y, self.c
        over, core = at(z, 1 - y, c), at(z, y, 1 - c)
        zs = partners(z)
        self.push(self.me, over, self.x_ref)
        for w in zs[::-1]:
            self.push(self.me, at(w, y, c), self.x_ref)
        self.push(self.me, core, self.x_ref)
        use(self.me)
        for k, w in enumerate([z] + zs):
            if k:
                shard = at(w, y, c)
                self.arrive(shard)
                self.push(shard, over, self.o_ref.at[shard])
                self.push(shard, core, self.o_ref.at[shard])
                use(shard)
        for w in [z] + zs:
            shard = at(w, 1 - y, c)
            self.arrive(shard)
            self.push(shard, core, self.o_ref.at[shard])
            use(shard)
        for w in [z] + zs:
            for v in (y, 1 - y):
                shard = at(w, v, 1 - c)
                self.arrive(shard)
                use(shard)
        for copy in self.sent:
            copy.wait_send()


def gather_kernel(x_ref, o_ref, send, recv):
    me, z, y, c = place()
    greet(z, y, c)
    o_ref[me] = x_ref[...]
    Gather(x_ref, o_ref, send, recv).run(lambda shard: None)


def gather(x, devices, tag):
    vmem = pl.BlockSpec(memory_space=pltpu.VMEM)
    return pl.pallas_call(
        gather_kernel,
        out_shape=jax.ShapeDtypeStruct((devices,) + x.shape, x.dtype),
        in_specs=[vmem],
        out_specs=vmem,
        scratch_shapes=[pltpu.SemaphoreType.DMA((15,)), pltpu.SemaphoreType.DMA((16,))],
        compiler_params=pltpu.CompilerParams(
            collective_id=tag, has_side_effects=True, vmem_limit_bytes=32 * 2**20
        ),
    )(x)


def merge_kernel(
    heads, rows, num_ref, st_ref, ow_ref, out_ref,
    in1, st1, acc1, sacc1, in2, st2, acc2, sacc2, in3, st3, att, full, weight,
    send, recv, gsend, grecv, wsem,
):
    me, z, y, c = place()
    fetch = pltpu.make_async_copy(ow_ref, weight, wsem)
    fetch.start()
    greet(z, y, c)
    over, core = at(z, 1 - y, c), at(z, y, 1 - c)
    order = partners(z)[::-1] + [z]
    started = []

    def ship(src, ssrc, dst, sdst, target):
        slot = len(started)
        for copy_src, copy_dst, lane in ((src, dst, 0), (ssrc, sdst, 1)):
            pltpu.make_async_remote_copy(
                src_ref=copy_src, dst_ref=copy_dst, send_sem=send.at[slot, lane], recv_sem=recv.at[slot, lane],
                device_id={"beam": target}, device_id_type=MESH,
            ).start()
        started.append((src, ssrc, dst, sdst, target))

    def handle(slot, lane):
        src, ssrc, dst, sdst, target = started[slot]
        return pltpu.make_async_remote_copy(
            src_ref=(src, ssrc)[lane], dst_ref=(dst, sdst)[lane], send_sem=send.at[slot, lane],
            recv_sem=recv.at[slot, lane], device_id={"beam": target}, device_id_type=MESH,
        )

    def landed(slot):
        handle(slot, 0).wait_recv()
        handle(slot, 1).wait_recv()

    def weigh(stats):
        top = stats[0][:heads]
        for item in stats[1:]:
            top = jnp.maximum(top, item[:heads])
        scale = [jnp.exp(item[:heads] - top) for item in stats]
        total = scale[0] * stats[0][heads:]
        for e, item in zip(scale[1:], stats[1:]):
            total = total + e * item[heads:]
        return top, scale, total

    def flip(top_half, low_half):
        return jnp.transpose(jnp.concatenate([top_half, low_half], 0))

    def merge(a, sa, b, sb, dst, sdst):
        top, scale, total = weigh([sa[...], sb[...]])
        sdst[...] = jnp.concatenate([top, total], 0)
        e = flip(scale[0], scale[1])
        for h in range(heads):
            part = pl.ds(h * rows, rows)
            dst[part, :] = (
                a[part, :].astype(jnp.float32) * e[:rows, h : h + 1]
                + b[part, :].astype(jnp.float32) * e[:rows, heads + h : heads + h + 1]
            ).astype(jnp.bfloat16)

    for v, base in ((1 - y, 0), (y, 4)):
        for k, w in enumerate(order):
            chunk = at(w, v, 1 - c)
            ship(num_ref.at[chunk], st_ref.at[chunk], in1.at[base + k], st1.at[base + k], core)
    for k, w in enumerate(order):
        chunk = at(w, 1 - y, c)
        landed(k)
        merge(num_ref.at[chunk], st_ref.at[chunk], in1.at[k], st1.at[k], acc1.at[k], sacc1.at[k])
        ship(acc1.at[k], sacc1.at[k], in2.at[k], st2.at[k], over)
    for k, w in enumerate(order):
        chunk = at(w, y, c)
        landed(4 + k)
        merge(num_ref.at[chunk], st_ref.at[chunk], in1.at[4 + k], st1.at[4 + k], acc1.at[4 + k], sacc1.at[4 + k])
    for k, w in enumerate(order):
        landed(8 + k)
        merge(acc1.at[4 + k], sacc1.at[4 + k], in2.at[k], st2.at[k], acc2.at[k], sacc2.at[k])
        if k < 3:
            ship(acc2.at[k], sacc2.at[k], in3.at[k], st3.at[k], at(w, y, c))
    for k in range(3):
        landed(12 + k)
    stats = [sacc2[3]] + [st3[k] for k in range(3)]
    top, scale, total = weigh(stats)
    e01, e23 = flip(scale[0], scale[1]), flip(scale[2], scale[3])
    below = flip(total, total)
    for h in range(heads):
        part = pl.ds(h * rows, rows)
        value = acc2[3, part, :].astype(jnp.float32) * e01[:rows, h : h + 1]
        for k, table, lane in ((0, e01, heads + h), (1, e23, h), (2, e23, heads + h)):
            value = value + in3[k, part, :].astype(jnp.float32) * table[:rows, lane : lane + 1]
        att[:, h * HEAD_DIM : (h + 1) * HEAD_DIM] = (value / below[:rows, h : h + 1]).astype(jnp.bfloat16)
    full[me] = att[...]
    fetch.wait()
    depth = heads * HEAD_DIM
    total = [None]

    def use(shard):
        term = jnp.dot(
            full[shard], weight[pl.ds(shard * depth, depth), :], preferred_element_type=jnp.float32
        )
        total[0] = term if total[0] is None else total[0] + term

    Gather(att, full, gsend, grecv).run(use)
    out_ref[...] = total[0].astype(jnp.bfloat16)
    for slot in range(len(started)):
        handle(slot, 0).wait_send()
        handle(slot, 1).wait_send()


def merge_and_project(num, stats, o_weight, heads, rows, tag):
    devices = num.shape[0]
    vmem = pl.BlockSpec(memory_space=pltpu.VMEM)
    chunk = num.shape[1:]
    depth, cols = o_weight.shape
    bf = lambda k: pltpu.VMEM((k,) + chunk, jnp.bfloat16)
    fl = lambda k: pltpu.VMEM((k,) + stats.shape[1:], jnp.float32)
    return pl.pallas_call(
        lambda *refs: merge_kernel(heads, rows, *refs),
        out_shape=jax.ShapeDtypeStruct((rows, cols), jnp.bfloat16),
        in_specs=[vmem, vmem, pl.BlockSpec(memory_space=pl.ANY)],
        out_specs=vmem,
        scratch_shapes=[
            bf(8), fl(8), bf(8), fl(8), bf(4), fl(4), bf(4), fl(4), bf(3), fl(3),
            pltpu.VMEM((rows, heads * HEAD_DIM), jnp.bfloat16),
            pltpu.VMEM((devices, rows, heads * HEAD_DIM), jnp.bfloat16),
            pltpu.VMEM((depth, cols), jnp.bfloat16),
            pltpu.SemaphoreType.DMA((15, 2)),
            pltpu.SemaphoreType.DMA((15, 2)),
            pltpu.SemaphoreType.DMA((15,)),
            pltpu.SemaphoreType.DMA((16,)),
            pltpu.SemaphoreType.DMA,
        ],
        compiler_params=pltpu.CompilerParams(
            collective_id=tag, has_side_effects=True, vmem_limit_bytes=40 * 2**20
        ),
    )(num, stats, o_weight)


def lineage_tables(parents, prefix_lens, tail_lens, rows_per_chip, devices):
    all_rows = parents.shape[1]
    row_ids = jnp.arange(all_rows, dtype=jnp.int32)
    ancestors = row_ids
    makers = []
    anc_steps, pos_steps, maker_steps = [], [], []
    base = prefix_lens[row_ids // BEAM_COUNT]
    for step in range(STEPS):
        hot = parents[step][:, None] == row_ids[None, :]
        pick = lambda item: jnp.sum(jnp.where(hot, item[None, :], 0), axis=1)
        ancestors = pick(ancestors)
        makers = [pick(item) for item in makers] + [row_ids]
        lens = jnp.sum(jnp.where(ancestors[:, None] == row_ids[None, :], tail_lens[None, :], 0), axis=1)
        anc_steps.append(ancestors)
        pos_steps.append(base + lens + step)
        maker_steps.append(jnp.stack(makers + [jnp.full_like(row_ids, -1)] * (STEPS - 1 - step), 0))

    def order(table):
        lead = table.shape[1:-1]
        table = table.reshape((STEPS,) + lead + (devices, rows_per_chip))
        table = jnp.moveaxis(table, -2, 0)
        table = jnp.moveaxis(table, 1, -2)
        return jnp.moveaxis(table, 0, -3).reshape(lead + (STEPS * all_rows,))

    return order(jnp.stack(anc_steps, 0)), order(jnp.stack(pos_steps, 0)), order(jnp.stack(maker_steps, 0))


def local(
    hidden,
    norm_gain,
    q_weight,
    q_bias,
    kv_weight,
    kv_bias,
    o_weight,
    prefix_key_cache,
    prefix_value_cache,
    prefix_index,
    prefix_lens,
    tail_key_cache,
    tail_value_cache,
    tail_lens,
    parents,
):
    devices = lax.axis_size("beam")
    me = lax.axis_index("beam")
    rpc = hidden.shape[1]
    width = hidden.shape[2]
    if devices != 16 or 2 * kv_weight.shape[2] != HEAD_DIM or STEPS * rpc > 8:
        return local_by_rows(
            hidden, norm_gain, q_weight, q_bias, kv_weight, kv_bias, o_weight, prefix_key_cache,
            prefix_value_cache, prefix_index, prefix_lens, tail_key_cache, tail_value_cache, tail_lens, parents,
        )
    own = STEPS * rpc
    rows = own * devices
    prompts = prefix_index.shape[0]
    ppr = rows // prompts
    heads = QUERY_HEADS // devices
    group = QUERY_HEADS // KEY_HEADS
    q_cols = q_weight.shape[1]
    kv_cols = kv_weight.shape[2]
    slab = prefix_key_cache.shape[1]
    tail = tail_key_cache.shape[1]
    score_scale = 1.0 / math.sqrt(HEAD_DIM)
    my_prompt = me * rpc // BEAM_COUNT
    anc, pos, made = lineage_tables(parents, prefix_lens, tail_lens, rpc, devices)

    x = hidden.astype(jnp.float32)
    normed = (x * lax.rsqrt(jnp.mean(x * x, axis=-1, keepdims=True) + EPS) * norm_gain).astype(jnp.bfloat16)
    normed = jnp.pad(normed.reshape(own, width), ((0, 8 - own), (0, 0)))
    normed = gather(normed, devices, 0).reshape(devices * 8, width)
    real = lambda v: v.reshape(devices, 8, v.shape[1])[:, :own].reshape(rows, v.shape[1])
    q = (jnp.dot(normed, q_weight, preferred_element_type=jnp.float32) + q_bias).astype(jnp.bfloat16)
    kv = jnp.dot(normed, kv_weight.reshape(width, 2 * kv_cols), preferred_element_type=jnp.float32)
    kv = (kv + kv_bias.reshape(2 * kv_cols)).astype(jnp.bfloat16)
    q, kv = real(q), real(kv)
    cosine, sine = rope_parts(pos, HEAD_DIM)
    cosine2 = jnp.concatenate([cosine, cosine], 1)
    sine2 = jnp.concatenate([-sine, sine], 1)

    def rotate(v):
        v = v.astype(jnp.float32)
        return (v * cosine2 + jnp.roll(v, HEAD_DIM // 2, axis=-1) * sine2).astype(jnp.bfloat16)

    pieces = [rotate(q[:, h * HEAD_DIM : (h + 1) * HEAD_DIM]) for h in range(heads)] + [kv]
    full = gather(jnp.stack(pieces, 0), devices, 1)
    query = full[:, :heads].reshape(KEY_HEADS, group, prompts, ppr, HEAD_DIM)
    mine6 = lax.dynamic_slice_in_dim(full[:, heads], me * own, own, 1).reshape(devices, own, 2, kv_cols)
    mine6 = jnp.transpose(mine6, (2, 1, 0, 3)).reshape(2, own, KEY_HEADS, HEAD_DIM)
    my_cos = lax.dynamic_slice_in_dim(cosine2, me * own, own, 0)[:, None]
    my_sin = lax.dynamic_slice_in_dim(sine2, me * own, own, 0)[:, None]
    fk = mine6[0].astype(jnp.float32)
    fk = (fk * my_cos + jnp.roll(fk, HEAD_DIM // 2, axis=-1) * my_sin).astype(jnp.bfloat16)
    fv = mine6[1]

    num, gmax, gsum = attend(
        query, fk, fv, prefix_key_cache, prefix_value_cache, prefix_index, prefix_lens,
        tail_key_cache, tail_value_cache, tail_lens, anc, made, me, my_prompt, rpc, score_scale,
    )
    stats = jnp.concatenate([gmax.reshape(devices, heads, rows), gsum.reshape(devices, heads, rows)], 1)
    stats = jnp.pad(stats, ((0, 0), (0, 0), (0, 128 - rows)))
    out = merge_and_project(num.reshape(devices, heads * rows, HEAD_DIM), stats, o_weight, heads, rows, 2)
    out = out.reshape(devices, STEPS, rpc, out.shape[1])
    return jnp.transpose(out, (1, 0, 2, 3)).reshape(STEPS, devices * rpc, out.shape[3])


def attend(
    query, fk, fv, prefix_keys, prefix_values, prefix_index, prefix_lens,
    tail_keys, tail_values, tail_lens, anc, made, me, my_prompt, rpc, score_scale,
):
    khs, group, prompts, ppr, hd = query.shape
    slab = prefix_keys.shape[1]
    tail = tail_keys.shape[1]
    own = fk.shape[0]
    rows = prompts * ppr
    first = me * rpc
    pk = jnp.take(prefix_keys, prefix_index, axis=0).reshape(prompts, slab, khs, hd)
    pv = jnp.take(prefix_values, prefix_index, axis=0).reshape(prompts, slab, khs, hd)
    s = jnp.einsum("kgpbd,pskd->kpgbs", query, pk, preferred_element_type=jnp.float32) * score_scale
    ok = (me * slab + jnp.arange(slab, dtype=jnp.int32))[None, :] < prefix_lens[:, None]
    ok = ok[None, :, None, None, :]
    s = jnp.where(ok, s, NEG)
    lq = lax.dynamic_index_in_dim(query, my_prompt, 2, keepdims=False).reshape(khs, group, ppr, hd)
    lanc = lax.dynamic_slice_in_dim(anc, my_prompt * ppr, ppr, 0)
    lmade = lax.dynamic_slice_in_dim(made, my_prompt * ppr, ppr, 1)
    own_lens = lax.dynamic_slice_in_dim(tail_lens, first, rpc, 0)
    slot = first + jnp.arange(rpc, dtype=jnp.int32)
    t_ok = (lanc[:, None] == slot[None, :])[:, :, None] & (
        jnp.arange(tail, dtype=jnp.int32)[None, None, :] < own_lens[None, :, None]
    )
    f_ok = lmade.T[:, :, None] == slot[None, None, :]
    l_ok = jnp.concatenate([t_ok.reshape(ppr, rpc * tail), f_ok.reshape(ppr, own)], 1)[None, None]
    lk = jnp.concatenate([tail_keys.reshape(rpc * tail, khs, hd), fk], 0)
    lv = jnp.concatenate([tail_values.reshape(rpc * tail, khs, hd), fv], 0)
    ls = jnp.einsum("kgbd,tkd->kgbt", lq, lk, preferred_element_type=jnp.float32) * score_scale
    ls = jnp.where(l_ok, ls, NEG)
    mine = (jnp.arange(prompts, dtype=jnp.int32) == my_prompt)[None, :, None, None]
    gmax = jnp.maximum(s.max(-1), jnp.where(mine, ls.max(-1)[:, None], NEG))
    lmax = lax.dynamic_index_in_dim(gmax, my_prompt, 1, keepdims=False)
    w = jnp.where(ok, jnp.exp(s - gmax[..., None]), 0.0)
    lw = jnp.where(l_ok, jnp.exp(ls - lmax[..., None]), 0.0)
    gsum = w.sum(-1) + jnp.where(mine, lw.sum(-1)[:, None], 0.0)
    num = jnp.einsum("kpgbs,pskd->kpgbd", w.astype(jnp.bfloat16), pv, preferred_element_type=jnp.float32)
    lnum = jnp.einsum("kgbt,tkd->kgbd", lw.astype(jnp.bfloat16), lv, preferred_element_type=jnp.float32)
    num = num + jnp.where(mine[..., None], lnum[:, None], 0.0)
    num = jnp.swapaxes(num.astype(jnp.bfloat16), 1, 2).reshape(khs * group, rows, hd)
    return num, jnp.swapaxes(gmax, 1, 2).reshape(khs * group, rows), jnp.swapaxes(gsum, 1, 2).reshape(khs * group, rows)


def solution(mesh):
    return jax.shard_map(
        local,
        mesh=mesh,
        in_specs=(
            P(None, ("grp", "beam"), None),
            P(),
            P(None, "beam"),
            P("beam"),
            P(None, None, "beam"),
            P(None, "beam"),
            P(None, "beam"),
            P("grp", "beam", None),
            P("grp", "beam", None),
            P("grp"),
            P("grp"),
            P(("grp", "beam"), None, None),
            P(("grp", "beam"), None, None),
            P("grp"),
            P(None, "grp"),
        ),
        out_specs=P(None, "grp", "beam"),
        check_vma=False,
    )
```

```python
import math

import jax
import jax.numpy as jnp
import numpy as np
from jax import lax
from jax.experimental import pallas as pl
from jax.experimental.pallas import tpu as pltpu
from jax.sharding import PartitionSpec as P

QUERY_HEADS = 64
KEY_HEADS = 8
HEAD_DIM = 128
BEAM_COUNT = 16
STEPS = 3


EPS = 1e-06
NEG = -1e30
ROPE_BASE = 1000000.0


def rope_parts(positions, head_size):
    half = head_size // 2
    freqs = np.power(ROPE_BASE, -np.arange(half) * 2.0 / head_size)
    angle = positions.astype(jnp.float32)[:, None] * jnp.asarray(freqs, jnp.float32)[None, :]
    return (jnp.cos(angle), jnp.sin(angle))


def apply_rotation(value_rows, cosine_table, sine_table):
    half = value_rows.shape[-1] // 2
    first = value_rows[..., :half]
    second = value_rows[..., half:]
    cosine_table = cosine_table[:, None, :]
    sine_table = sine_table[:, None, :]
    return jnp.concatenate(
        [first * cosine_table - second * sine_table, second * cosine_table + first * sine_table],
        axis=-1,
    )


def local_by_rows(
    hidden,
    norm_gain,
    q_weight,
    q_bias,
    kv_weight,
    kv_bias,
    o_weight,
    prefix_key_cache,
    prefix_value_cache,
    prefix_index,
    prefix_lens,
    tail_key_cache,
    tail_value_cache,
    tail_lens,
    parents,
):
    devices = lax.axis_size("beam")
    me = lax.axis_index("beam")
    rows_per_chip = hidden.shape[1]
    width = hidden.shape[2]
    all_rows = rows_per_chip * devices
    prompt_batch = all_rows // BEAM_COUNT
    head_group = QUERY_HEADS // KEY_HEADS
    q_width = QUERY_HEADS * HEAD_DIM
    q_cols = q_weight.shape[1]
    kv_cols = kv_weight.shape[2]
    prefix_slice = prefix_key_cache.shape[1]
    tail_cache = tail_key_cache.shape[1]
    score_scale = 1.0 / math.sqrt(HEAD_DIM)
    row_ids = jnp.arange(all_rows, dtype=jnp.int32)
    prompt_of = row_ids // BEAM_COUNT
    first_row = me * rows_per_chip
    my_prompt = first_row // BEAM_COUNT
    slot_ids = first_row + jnp.arange(rows_per_chip, dtype=jnp.int32)
    mine = (jnp.arange(prompt_batch, dtype=jnp.int32) == my_prompt)[:, None, None, None]
    joint = jnp.concatenate([q_weight, kv_weight.reshape(width, 2 * kv_cols)], axis=1)
    joint_bias = jnp.concatenate([q_bias, kv_bias.reshape(2 * kv_cols)])
    slice_keys = jnp.take(prefix_key_cache, prefix_index, axis=0).reshape(
        prompt_batch, prefix_slice, KEY_HEADS, HEAD_DIM
    )
    slice_values = jnp.take(prefix_value_cache, prefix_index, axis=0).reshape(
        prompt_batch, prefix_slice, KEY_HEADS, HEAD_DIM
    )
    slab_ok = (me * prefix_slice + jnp.arange(prefix_slice, dtype=jnp.int32))[
        None, :
    ] < prefix_lens[:, None]
    slab_ok = slab_ok[:, None, None, None, :]
    tail_key_rows = tail_key_cache.reshape(rows_per_chip, tail_cache, KEY_HEADS, HEAD_DIM)
    tail_value_rows = tail_value_cache.reshape(rows_per_chip, tail_cache, KEY_HEADS, HEAD_DIM)
    own_lens = lax.dynamic_slice_in_dim(tail_lens, first_row, rows_per_chip, 0)
    tail_ok = jnp.arange(tail_cache, dtype=jnp.int32)[None, :] < own_lens[:, None]
    ancestors = row_ids
    makers = []
    fresh_keys = []
    current_values = []
    results = []
    for step in range(STEPS):
        chosen = parents[step]
        ancestors = ancestors[chosen]
        makers = [item[chosen] for item in makers] + [row_ids]
        value_rows = lax.all_gather(hidden[step], "beam", axis=0, tiled=True).astype(jnp.float32)
        normed = (
            value_rows
            * lax.rsqrt(jnp.mean(value_rows * value_rows, axis=-1, keepdims=True) + EPS)
            * norm_gain
        ).astype(jnp.bfloat16)
        projected = jnp.dot(normed, joint, preferred_element_type=jnp.float32) + joint_bias
        q_part = projected[:, :q_cols].astype(jnp.bfloat16)
        kv_part = projected[:, q_cols:].astype(jnp.bfloat16).reshape(all_rows, 2, kv_cols)
        positions = prefix_lens[prompt_of] + tail_lens[ancestors] + step
        cosine_table, sine_table = rope_parts(positions, HEAD_DIM)
        q_full, kv_full = (
            lax.all_gather(q_part[:, None, :], "beam", axis=2, tiled=True),
            lax.all_gather(kv_part, "beam", axis=2, tiled=True),
        )
        q_all = q_full[:, 0, :]
        owned_key_value = lax.dynamic_slice_in_dim(kv_full, first_row, rows_per_chip, 0)
        rotated_rows = apply_rotation(
            q_all.astype(jnp.float32).reshape(all_rows, QUERY_HEADS, HEAD_DIM),
            cosine_table,
            sine_table,
        ).astype(jnp.bfloat16)
        local_cosine = lax.dynamic_slice_in_dim(cosine_table, first_row, rows_per_chip, 0)
        local_sine = lax.dynamic_slice_in_dim(sine_table, first_row, rows_per_chip, 0)
        new_key = apply_rotation(
            owned_key_value[:, 0].astype(jnp.float32).reshape(rows_per_chip, KEY_HEADS, HEAD_DIM),
            local_cosine,
            local_sine,
        ).astype(jnp.bfloat16)
        fresh_keys.append(new_key)
        current_values.append(owned_key_value[:, 1].reshape(rows_per_chip, KEY_HEADS, HEAD_DIM))
        query_rows = rotated_rows.reshape(prompt_batch, BEAM_COUNT, KEY_HEADS, head_group, HEAD_DIM)
        pre_scores = (
            jnp.einsum(
                "pbkgd,pskd->pbkgs", query_rows, slice_keys, preferred_element_type=jnp.float32
            )
            * score_scale
        )
        pre_scores = jnp.where(slab_ok, pre_scores, NEG)
        local_q = lax.dynamic_index_in_dim(query_rows, my_prompt, 0, keepdims=False)
        local_anc = lax.dynamic_slice_in_dim(ancestors, my_prompt * BEAM_COUNT, BEAM_COUNT, 0)
        t_scores = (
            jnp.einsum(
                "bkgd,itkd->bkgit", local_q, tail_key_rows, preferred_element_type=jnp.float32
            )
            * score_scale
        )
        t_valid = (local_anc[:, None] == slot_ids[None, :])[:, None, None, :, None] & tail_ok[
            None, None, None, :, :
        ]
        t_scores = jnp.where(t_valid, t_scores, NEG)
        f_keys = jnp.stack(fresh_keys, 0)
        f_values = jnp.stack(current_values, 0)
        local_made = jnp.stack(
            [
                lax.dynamic_slice_in_dim(item, my_prompt * BEAM_COUNT, BEAM_COUNT, 0)
                for item in makers
            ],
            1,
        )
        f_valid = (local_made[:, :, None] == slot_ids[None, None, :])[:, None, None, :, :]
        f_scores = (
            jnp.einsum("bkgd,jikd->bkgji", local_q, f_keys, preferred_element_type=jnp.float32)
            * score_scale
        )
        f_scores = jnp.where(f_valid, f_scores, NEG)
        local_max = jnp.maximum(t_scores.max(axis=(3, 4)), f_scores.max(axis=(3, 4)))
        pre_max = pre_scores.max(-1)
        group_maximum = jnp.where(mine, jnp.maximum(pre_max, local_max[None]), pre_max)
        mine_max = lax.dynamic_index_in_dim(group_maximum, my_prompt, 0, keepdims=False)
        pre_w = jnp.where(slab_ok, jnp.exp(pre_scores - group_maximum[..., None]), 0.0)
        totals = pre_w.sum(-1)
        numer = jnp.einsum(
            "pbkgs,pskd->pbkgd",
            pre_w.astype(jnp.bfloat16),
            slice_values,
            preferred_element_type=jnp.float32,
        )
        t_w = jnp.where(t_valid, jnp.exp(t_scores - mine_max[..., None, None]), 0.0)
        f_w = jnp.where(f_valid, jnp.exp(f_scores - mine_max[..., None, None]), 0.0)
        local_total = t_w.sum(axis=(3, 4)) + f_w.sum(axis=(3, 4))
        local_num = jnp.einsum(
            "bkgit,itkd->bkgd",
            t_w.astype(jnp.bfloat16),
            tail_value_rows,
            preferred_element_type=jnp.float32,
        )
        local_num = local_num + jnp.einsum(
            "bkgji,jikd->bkgd",
            f_w.astype(jnp.bfloat16),
            f_values,
            preferred_element_type=jnp.float32,
        )
        totals = jnp.where(mine, totals + local_total[None], totals)
        numer = jnp.where(mine[..., None], numer + local_num[None], numer)
        sending = numer.astype(jnp.bfloat16).reshape(devices, rows_per_chip, q_width)
        parts = lax.all_to_all(sending, "beam", split_axis=0, concat_axis=0, tiled=True)
        maxima, sums = (
            lax.all_to_all(
                group_maximum.reshape(devices, rows_per_chip, QUERY_HEADS),
                "beam",
                split_axis=0,
                concat_axis=0,
                tiled=True,
            ),
            lax.all_to_all(
                totals.reshape(devices, rows_per_chip, QUERY_HEADS),
                "beam",
                split_axis=0,
                concat_axis=0,
                tiled=True,
            ),
        )
        top = maxima.max(0)
        factors = jnp.exp(maxima - top[None])
        denom = (factors * sums).sum(0)
        combined = jnp.einsum(
            "srh,srhd->rhd",
            factors,
            parts.reshape(devices, rows_per_chip, QUERY_HEADS, HEAD_DIM),
            preferred_element_type=jnp.float32,
        )
        attention = (
            (combined / denom[..., None]).reshape(rows_per_chip, q_width).astype(jnp.bfloat16)
        )
        out_cols = jnp.dot(
            lax.all_gather(attention, "beam", axis=0, tiled=True),
            o_weight,
            preferred_element_type=jnp.float32,
        )
        results.append(out_cols.astype(jnp.bfloat16))
    return jnp.stack(results, 0)


MESH = pl.DeviceIdType.MESH


def place():
    me = lax.axis_index("beam")
    return me, me // 4, me // 2 % 2, me % 2


def at(z, y, c):
    return (z * 2 + y) * 2 + c


def partners(z):
    return [z + 1 - 2 * (z % 2), (z + 2) % 4, 3 - z]


def greet(z, y, c):
    barrier = pltpu.get_barrier_semaphore()
    others = [at(w, y, c) for w in partners(z)] + [at(z, 1 - y, c), at(z, y, 1 - c)]
    for other in others:
        pl.semaphore_signal(barrier, inc=1, device_id={"beam": other}, device_id_type=MESH)
    pl.semaphore_wait(barrier, len(others))


class Gather:
    def __init__(self, x_ref, o_ref, send, recv):
        self.x_ref, self.o_ref, self.send, self.recv = x_ref, o_ref, send, recv
        self.me, self.z, self.y, self.c = place()
        self.sent = []

    def push(self, shard, target, src):
        copy = pltpu.make_async_remote_copy(
            src_ref=src,
            dst_ref=self.o_ref.at[shard],
            send_sem=self.send.at[len(self.sent)],
            recv_sem=self.recv.at[shard],
            device_id={"beam": target},
            device_id_type=MESH,
        )
        copy.start()
        self.sent.append(copy)

    def arrive(self, shard):
        pltpu.make_async_remote_copy(
            src_ref=self.o_ref.at[shard],
            dst_ref=self.o_ref.at[shard],
            send_sem=self.send.at[0],
            recv_sem=self.recv.at[shard],
            device_id={"beam": at(self.z, self.y, 1 - self.c)},
            device_id_type=MESH,
        ).wait_recv()

    def run(self, use):
        z, y, c = self.z, self.y, self.c
        over, core = at(z, 1 - y, c), at(z, y, 1 - c)
        zs = partners(z)
        self.push(self.me, over, self.x_ref)
        for w in zs[::-1]:
            self.push(self.me, at(w, y, c), self.x_ref)
        self.push(self.me, core, self.x_ref)
        use(self.me)
        for k, w in enumerate([z] + zs):
            if k:
                shard = at(w, y, c)
                self.arrive(shard)
                self.push(shard, over, self.o_ref.at[shard])
                self.push(shard, core, self.o_ref.at[shard])
                use(shard)
        for w in [z] + zs:
            shard = at(w, 1 - y, c)
            self.arrive(shard)
            self.push(shard, core, self.o_ref.at[shard])
            use(shard)
        for w in [z] + zs:
            for v in (y, 1 - y):
                shard = at(w, v, 1 - c)
                self.arrive(shard)
                use(shard)
        for copy in self.sent:
            copy.wait_send()


def gather_kernel(x_ref, o_ref, send, recv):
    me, z, y, c = place()
    greet(z, y, c)
    o_ref[me] = x_ref[...]
    Gather(x_ref, o_ref, send, recv).run(lambda shard: None)


def gather(x, devices, tag):
    vmem = pl.BlockSpec(memory_space=pltpu.VMEM)
    return pl.pallas_call(
        gather_kernel,
        out_shape=jax.ShapeDtypeStruct((devices,) + x.shape, x.dtype),
        in_specs=[vmem],
        out_specs=vmem,
        scratch_shapes=[pltpu.SemaphoreType.DMA((15,)), pltpu.SemaphoreType.DMA((16,))],
        compiler_params=pltpu.CompilerParams(
            collective_id=tag, has_side_effects=True, vmem_limit_bytes=32 * 2**20
        ),
    )(x)


def merge_kernel(
    heads, rows, num_ref, st_ref, ow_ref, out_ref,
    in1, st1, acc1, sacc1, in2, st2, acc2, sacc2, in3, st3, att, full, weight,
    send, recv, gsend, grecv, wsem,
):
    me, z, y, c = place()
    fetch = pltpu.make_async_copy(ow_ref, weight, wsem)
    fetch.start()
    greet(z, y, c)
    over, core = at(z, 1 - y, c), at(z, y, 1 - c)
    order = partners(z)[::-1] + [z]
    started = []

    def ship(src, ssrc, dst, sdst, target):
        slot = len(started)
        for copy_src, copy_dst, lane in ((src, dst, 0), (ssrc, sdst, 1)):
            pltpu.make_async_remote_copy(
                src_ref=copy_src, dst_ref=copy_dst, send_sem=send.at[slot, lane], recv_sem=recv.at[slot, lane],
                device_id={"beam": target}, device_id_type=MESH,
            ).start()
        started.append((src, ssrc, dst, sdst, target))

    def handle(slot, lane):
        src, ssrc, dst, sdst, target = started[slot]
        return pltpu.make_async_remote_copy(
            src_ref=(src, ssrc)[lane], dst_ref=(dst, sdst)[lane], send_sem=send.at[slot, lane],
            recv_sem=recv.at[slot, lane], device_id={"beam": target}, device_id_type=MESH,
        )

    def landed(slot):
        handle(slot, 0).wait_recv()
        handle(slot, 1).wait_recv()

    def weigh(stats):
        top = stats[0][:heads]
        for item in stats[1:]:
            top = jnp.maximum(top, item[:heads])
        scale = [jnp.exp(item[:heads] - top) for item in stats]
        total = scale[0] * stats[0][heads:]
        for e, item in zip(scale[1:], stats[1:]):
            total = total + e * item[heads:]
        return top, scale, total

    def flip(top_half, low_half):
        return jnp.transpose(jnp.concatenate([top_half, low_half], 0))

    def merge(a, sa, b, sb, dst, sdst):
        top, scale, total = weigh([sa[...], sb[...]])
        sdst[...] = jnp.concatenate([top, total], 0)
        e = flip(scale[0], scale[1])
        for h in range(heads):
            part = pl.ds(h * rows, rows)
            dst[part, :] = (
                a[part, :].astype(jnp.float32) * e[:rows, h : h + 1]
                + b[part, :].astype(jnp.float32) * e[:rows, heads + h : heads + h + 1]
            ).astype(jnp.bfloat16)

    for v, base in ((1 - y, 0), (y, 4)):
        for k, w in enumerate(order):
            chunk = at(w, v, 1 - c)
            ship(num_ref.at[chunk], st_ref.at[chunk], in1.at[base + k], st1.at[base + k], core)
    for k, w in enumerate(order):
        chunk = at(w, 1 - y, c)
        landed(k)
        merge(num_ref.at[chunk], st_ref.at[chunk], in1.at[k], st1.at[k], acc1.at[k], sacc1.at[k])
        ship(acc1.at[k], sacc1.at[k], in2.at[k], st2.at[k], over)
    for k, w in enumerate(order):
        chunk = at(w, y, c)
        landed(4 + k)
        merge(num_ref.at[chunk], st_ref.at[chunk], in1.at[4 + k], st1.at[4 + k], acc1.at[4 + k], sacc1.at[4 + k])
    for k, w in enumerate(order):
        landed(8 + k)
        merge(acc1.at[4 + k], sacc1.at[4 + k], in2.at[k], st2.at[k], acc2.at[k], sacc2.at[k])
        if k < 3:
            ship(acc2.at[k], sacc2.at[k], in3.at[k], st3.at[k], at(w, y, c))
    for k in range(3):
        landed(12 + k)
    stats = [sacc2[3]] + [st3[k] for k in range(3)]
    top, scale, total = weigh(stats)
    e01, e23 = flip(scale[0], scale[1]), flip(scale[2], scale[3])
    below = flip(total, total)
    for h in range(heads):
        part = pl.ds(h * rows, rows)
        value = acc2[3, part, :].astype(jnp.float32) * e01[:rows, h : h + 1]
        for k, table, lane in ((0, e01, heads + h), (1, e23, h), (2, e23, heads + h)):
            value = value + in3[k, part, :].astype(jnp.float32) * table[:rows, lane : lane + 1]
        att[:, h * HEAD_DIM : (h + 1) * HEAD_DIM] = (value / below[:rows, h : h + 1]).astype(jnp.bfloat16)
    full[me] = att[...]
    fetch.wait()
    depth = heads * HEAD_DIM
    total = [None]

    def use(shard):
        term = jnp.dot(
            full[shard], weight[pl.ds(shard * depth, depth), :], preferred_element_type=jnp.float32
        )
        total[0] = term if total[0] is None else total[0] + term

    Gather(att, full, gsend, grecv).run(use)
    out_ref[...] = total[0].astype(jnp.bfloat16)
    for slot in range(len(started)):
        handle(slot, 0).wait_send()
        handle(slot, 1).wait_send()


def merge_and_project(num, stats, o_weight, heads, rows, tag):
    devices = num.shape[0]
    vmem = pl.BlockSpec(memory_space=pltpu.VMEM)
    chunk = num.shape[1:]
    depth, cols = o_weight.shape
    bf = lambda k: pltpu.VMEM((k,) + chunk, jnp.bfloat16)
    fl = lambda k: pltpu.VMEM((k,) + stats.shape[1:], jnp.float32)
    return pl.pallas_call(
        lambda *refs: merge_kernel(heads, rows, *refs),
        out_shape=jax.ShapeDtypeStruct((rows, cols), jnp.bfloat16),
        in_specs=[vmem, vmem, pl.BlockSpec(memory_space=pl.ANY)],
        out_specs=vmem,
        scratch_shapes=[
            bf(8), fl(8), bf(8), fl(8), bf(4), fl(4), bf(4), fl(4), bf(3), fl(3),
            pltpu.VMEM((rows, heads * HEAD_DIM), jnp.bfloat16),
            pltpu.VMEM((devices, rows, heads * HEAD_DIM), jnp.bfloat16),
            pltpu.VMEM((depth, cols), jnp.bfloat16),
            pltpu.SemaphoreType.DMA((15, 2)),
            pltpu.SemaphoreType.DMA((15, 2)),
            pltpu.SemaphoreType.DMA((15,)),
            pltpu.SemaphoreType.DMA((16,)),
            pltpu.SemaphoreType.DMA,
        ],
        compiler_params=pltpu.CompilerParams(
            collective_id=tag, has_side_effects=True, vmem_limit_bytes=40 * 2**20
        ),
    )(num, stats, o_weight)


def attend_kernel(
    own, scale, x_ref, pk_ref, pv_ref, tk_ref, tv_ref, pok_ref, lok_ref, cs_ref, sn_ref,
    num_ref, st_ref, full, column, send, recv,
):
    me, z, y, c = place()
    greet(z, y, c)
    full[me] = x_ref[...]
    column[...] = jnp.zeros_like(column)
    over, core = at(z, 1 - y, c), at(z, y, 1 - c)
    heads = x_ref.shape[0] - 1
    rows = x_ref.shape[1]
    ppr = rows // 2
    tail = tk_ref.shape[0]
    my_prompt = me // 8
    group = 2 * heads

    def push(slot, shard, target, src):
        pltpu.make_async_remote_copy(
            src_ref=src, dst_ref=full.at[shard], send_sem=send.at[slot], recv_sem=recv.at[shard],
            device_id={"beam": target}, device_id_type=MESH,
        ).start()

    def arrive(shard):
        pltpu.make_async_remote_copy(
            src_ref=full.at[shard], dst_ref=full.at[shard], send_sem=send.at[0], recv_sem=recv.at[shard],
            device_id={"beam": core}, device_id_type=MESH,
        ).wait_recv()

    zs = partners(z)
    push(0, me, over, x_ref)
    for k in (2, 1, 0):
        push(1 + k, me, at(zs[k], y, c), x_ref)
    push(4, me, core, x_ref)
    for k, w in enumerate(zs):
        shard = at(w, y, c)
        arrive(shard)
        push(5 + 2 * k, shard, over, full.at[shard])
        push(6 + 2 * k, shard, core, full.at[shard])

    lane = lax.broadcasted_iota(jnp.int32, (16, HEAD_DIM), 1)
    pick_row = lax.broadcasted_iota(jnp.int32, (16, rows), 0)
    pick_col = lax.broadcasted_iota(jnp.int32, (16, rows), 1)
    hot = jnp.where((pick_col == me * own + pick_row) & (pick_row < own), 1.0, 0.0).astype(jnp.bfloat16)
    wide = lax.broadcasted_iota(jnp.int32, (ppr, 128), 1)
    contract = (((1,), (1,)), ((), ()))

    def queries(k, prompt):
        start = pl.multiple_of(prompt * ppr, 16)
        return jnp.concatenate(
            [full[2 * k + g // heads, g % heads, pl.ds(start, ppr), :] for g in range(group)], 0
        )

    def write(k, prompt, num, top, total):
        start = pl.multiple_of(prompt * ppr, 16)
        num = num.astype(jnp.bfloat16)
        table = jnp.zeros((ppr, 128), jnp.float32)
        for g in range(group):
            part = slice(g * ppr, (g + 1) * ppr)
            place_at = pl.multiple_of(g % heads * rows + prompt * ppr, 16)
            num_ref[2 * k + g // heads, pl.ds(place_at, ppr), :] = num[part]
            base = g // heads * 2 * heads + g % heads
            table = jnp.where(wide == base, top[part], table)
            table = jnp.where(wide == base + heads, total[part], table)
        column[pl.ds(start, ppr), :] = table

    def one(i, carry):
        w = (z // 2 + i % 4 // 2) % 2 * 2 + (z + i) % 2
        v = (y + i // 4) % 2

        @pl.when(i < 4)
        def _():
            shard = at(w, 1 - y, c)
            arrive(shard)
            push(11 + i, shard, core, full.at[shard])

        arrive(at(w, v, 1 - c))
        k = w * 2 + v
        cols = pl.ds(pl.multiple_of(k * HEAD_DIM, HEAD_DIM), HEAD_DIM)
        lo = jnp.dot(hot, full[2 * k, heads], preferred_element_type=jnp.float32)
        hi = jnp.dot(hot, full[2 * k + 1, heads], preferred_element_type=jnp.float32)
        key = jnp.where(lane < HEAD_DIM // 2, lo, pltpu.roll(hi, HEAD_DIM // 2, 1))
        value = jnp.where(lane < HEAD_DIM // 2, pltpu.roll(lo, HEAD_DIM // 2, 1), hi)
        key = key * cs_ref[...] + pltpu.roll(key, HEAD_DIM // 2, 1) * sn_ref[...]
        blank = jnp.zeros((128 - 16, HEAD_DIM), jnp.bfloat16)
        key = jnp.concatenate([key.astype(jnp.bfloat16), blank], 0)
        value = jnp.concatenate([value.astype(jnp.bfloat16), blank], 0)

        def prefix(prompt, q):
            keys = pk_ref[prompt, :, cols]
            s = lax.dot_general(q, keys, contract, preferred_element_type=jnp.float32) * scale
            ok = pok_ref[prompt][:1] > 0.0
            return jnp.where(ok, s, NEG), ok

        q = queries(k, 1 - my_prompt)
        s, ok = prefix(1 - my_prompt, q)
        top = jnp.max(s, axis=1, keepdims=True)
        e = jnp.where(ok, jnp.exp(s - top), 0.0)
        num = jnp.dot(e.astype(jnp.bfloat16), pv_ref[1 - my_prompt, :, cols], preferred_element_type=jnp.float32)
        write(k, 1 - my_prompt, num, top, jnp.sum(e, axis=1, keepdims=True))

        q = queries(k, my_prompt)
        s, ok = prefix(my_prompt, q)
        ls = jnp.concatenate(
            [
                lax.dot_general(q, tk_ref[:, cols], contract, preferred_element_type=jnp.float32),
                lax.dot_general(q, key, contract, preferred_element_type=jnp.float32),
            ],
            1,
        )
        lok = jnp.concatenate([lok_ref[...]] * group, 0) > 0.0
        ls = jnp.where(lok, ls * scale, NEG)
        top = jnp.maximum(jnp.max(s, axis=1, keepdims=True), jnp.max(ls, axis=1, keepdims=True))
        e = jnp.where(ok, jnp.exp(s - top), 0.0)
        le = jnp.where(lok, jnp.exp(ls - top), 0.0)
        total = jnp.sum(e, axis=1, keepdims=True) + jnp.sum(le, axis=1, keepdims=True)
        le = le.astype(jnp.bfloat16)
        num = jnp.dot(e.astype(jnp.bfloat16), pv_ref[my_prompt, :, cols], preferred_element_type=jnp.float32)
        num = num + jnp.dot(le[:, :tail], tv_ref[:, cols], preferred_element_type=jnp.float32)
        num = num + jnp.dot(le[:, tail:], value, preferred_element_type=jnp.float32)
        write(k, my_prompt, num, top, total)

        flat = jnp.transpose(column[...])
        st_ref[2 * k] = flat[: 2 * heads]
        st_ref[2 * k + 1] = flat[2 * heads : 4 * heads]
        return carry

    lax.fori_loop(0, 8, one, 0)
    for slot in range(15):
        pltpu.make_async_remote_copy(
            src_ref=x_ref, dst_ref=full.at[0], send_sem=send.at[slot], recv_sem=recv.at[0],
            device_id={"beam": core}, device_id_type=MESH,
        ).wait_send()


def gather_and_attend(pieces, pk, pv, tk, tv, pok, lok, cs, sn, own, scale, devices, tag):
    vmem = pl.BlockSpec(memory_space=pltpu.VMEM)
    heads, rows = pieces.shape[0] - 1, pieces.shape[1]
    return pl.pallas_call(
        lambda *refs: attend_kernel(own, scale, *refs),
        out_shape=[
            jax.ShapeDtypeStruct((devices, heads * rows, HEAD_DIM), jnp.bfloat16),
            jax.ShapeDtypeStruct((devices, 2 * heads, 128), jnp.float32),
        ],
        in_specs=[vmem] * 9,
        out_specs=[vmem, vmem],
        scratch_shapes=[
            pltpu.VMEM((devices,) + pieces.shape, jnp.bfloat16),
            pltpu.VMEM((128, 128), jnp.float32),
            pltpu.SemaphoreType.DMA((15,)),
            pltpu.SemaphoreType.DMA((16,)),
        ],
        compiler_params=pltpu.CompilerParams(
            collective_id=tag, has_side_effects=True, vmem_limit_bytes=40 * 2**20
        ),
    )(pieces, pk, pv, tk, tv, pok, lok, cs, sn)


def lineage_tables(parents, prefix_lens, tail_lens, rows_per_chip, devices):
    all_rows = parents.shape[1]
    row_ids = jnp.arange(all_rows, dtype=jnp.int32)
    ancestors = row_ids
    makers = []
    anc_steps, pos_steps, maker_steps = [], [], []
    base = prefix_lens[row_ids // BEAM_COUNT]
    for step in range(STEPS):
        hot = parents[step][:, None] == row_ids[None, :]
        pick = lambda item: jnp.sum(jnp.where(hot, item[None, :], 0), axis=1)
        ancestors = pick(ancestors)
        makers = [pick(item) for item in makers] + [row_ids]
        lens = jnp.sum(jnp.where(ancestors[:, None] == row_ids[None, :], tail_lens[None, :], 0), axis=1)
        anc_steps.append(ancestors)
        pos_steps.append(base + lens + step)
        maker_steps.append(jnp.stack(makers + [jnp.full_like(row_ids, -1)] * (STEPS - 1 - step), 0))

    def order(table):
        lead = table.shape[1:-1]
        table = table.reshape((STEPS,) + lead + (devices, rows_per_chip))
        table = jnp.moveaxis(table, -2, 0)
        table = jnp.moveaxis(table, 1, -2)
        return jnp.moveaxis(table, 0, -3).reshape(lead + (STEPS * all_rows,))

    return order(jnp.stack(anc_steps, 0)), order(jnp.stack(pos_steps, 0)), order(jnp.stack(maker_steps, 0))


def local(
    hidden,
    norm_gain,
    q_weight,
    q_bias,
    kv_weight,
    kv_bias,
    o_weight,
    prefix_key_cache,
    prefix_value_cache,
    prefix_index,
    prefix_lens,
    tail_key_cache,
    tail_value_cache,
    tail_lens,
    parents,
):
    devices = lax.axis_size("beam")
    me = lax.axis_index("beam")
    rpc = hidden.shape[1]
    width = hidden.shape[2]
    if devices != 16 or 2 * kv_weight.shape[2] != HEAD_DIM or STEPS * rpc > 8 or prefix_index.shape[0] != 2:
        return local_by_rows(
            hidden, norm_gain, q_weight, q_bias, kv_weight, kv_bias, o_weight, prefix_key_cache,
            prefix_value_cache, prefix_index, prefix_lens, tail_key_cache, tail_value_cache, tail_lens, parents,
        )
    own = STEPS * rpc
    rows = own * devices
    prompts = prefix_index.shape[0]
    ppr = rows // prompts
    heads = QUERY_HEADS // devices
    group = QUERY_HEADS // KEY_HEADS
    q_cols = q_weight.shape[1]
    kv_cols = kv_weight.shape[2]
    slab = prefix_key_cache.shape[1]
    tail = tail_key_cache.shape[1]
    score_scale = 1.0 / math.sqrt(HEAD_DIM)
    my_prompt = me * rpc // BEAM_COUNT
    anc, pos, made = lineage_tables(parents, prefix_lens, tail_lens, rpc, devices)

    x = hidden.astype(jnp.float32)
    normed = (x * lax.rsqrt(jnp.mean(x * x, axis=-1, keepdims=True) + EPS) * norm_gain).astype(jnp.bfloat16)
    normed = jnp.pad(normed.reshape(own, width), ((0, 8 - own), (0, 0)))
    normed = gather(normed, devices, 0).reshape(devices * 8, width)
    real = lambda v: v.reshape(devices, 8, v.shape[1])[:, :own].reshape(rows, v.shape[1])
    q = (jnp.dot(normed, q_weight, preferred_element_type=jnp.float32) + q_bias).astype(jnp.bfloat16)
    kv = jnp.dot(normed, kv_weight.reshape(width, 2 * kv_cols), preferred_element_type=jnp.float32)
    kv = (kv + kv_bias.reshape(2 * kv_cols)).astype(jnp.bfloat16)
    q, kv = real(q), real(kv)
    cosine, sine = rope_parts(pos, HEAD_DIM)
    cosine2 = jnp.concatenate([cosine, cosine], 1)
    sine2 = jnp.concatenate([-sine, sine], 1)

    def rotate(v):
        v = v.astype(jnp.float32)
        return (v * cosine2 + jnp.roll(v, HEAD_DIM // 2, axis=-1) * sine2).astype(jnp.bfloat16)

    pieces = [rotate(q[:, h * HEAD_DIM : (h + 1) * HEAD_DIM]) for h in range(heads)] + [kv]
    first = me * rpc
    slot = first + jnp.arange(rpc, dtype=jnp.int32)
    lanc = lax.dynamic_slice_in_dim(anc, my_prompt * ppr, ppr, 0)
    lmade = lax.dynamic_slice_in_dim(made, my_prompt * ppr, ppr, 1)
    own_lens = lax.dynamic_slice_in_dim(tail_lens, first, rpc, 0)
    t_ok = (lanc[:, None] == slot[None, :])[:, :, None] & (
        jnp.arange(tail, dtype=jnp.int32)[None, None, :] < own_lens[None, :, None]
    )
    f_ok = lmade.T[:, :, None] == slot[None, None, :]
    lok = jnp.concatenate([t_ok.reshape(ppr, rpc * tail), f_ok.reshape(ppr, own)], 1).astype(jnp.float32)
    lok = jnp.pad(lok, ((0, 0), (0, 128 - own)))
    pok = (me * slab + jnp.arange(slab, dtype=jnp.int32))[None, :] < prefix_lens[:, None]
    pok = jnp.broadcast_to(pok.astype(jnp.float32)[:, None], (prompts, 8, slab))
    my_cos = jnp.pad(lax.dynamic_slice_in_dim(cosine2, me * own, own, 0), ((0, 16 - own), (0, 0)))
    my_sin = jnp.pad(lax.dynamic_slice_in_dim(sine2, me * own, own, 0), ((0, 16 - own), (0, 0)))
    num, stats = gather_and_attend(
        jnp.stack(pieces, 0),
        jnp.take(prefix_key_cache, prefix_index, axis=0, mode="clip"),
        jnp.take(prefix_value_cache, prefix_index, axis=0, mode="clip"),
        tail_key_cache.reshape(rpc * tail, -1),
        tail_value_cache.reshape(rpc * tail, -1),
        pok, lok, my_cos, my_sin, own, score_scale, devices, 1,
    )
    out = merge_and_project(num, stats, o_weight, heads, rows, 2)
    out = out.reshape(devices, STEPS, rpc, out.shape[1])
    return jnp.transpose(out, (1, 0, 2, 3)).reshape(STEPS, devices * rpc, out.shape[3])


def solution(mesh):
    return jax.shard_map(
        local,
        mesh=mesh,
        in_specs=(
            P(None, ("grp", "beam"), None),
            P(),
            P(None, "beam"),
            P("beam"),
            P(None, None, "beam"),
            P(None, "beam"),
            P(None, "beam"),
            P("grp", "beam", None),
            P("grp", "beam", None),
            P("grp"),
            P("grp"),
            P(("grp", "beam"), None, None),
            P(("grp", "beam"), None, None),
            P("grp"),
            P(None, "grp"),
        ),
        out_specs=P(None, "grp", "beam"),
        check_vma=False,
    )
```

```python
import math

import jax
import jax.numpy as jnp
import numpy as np
from jax import lax
from jax.experimental import pallas as pl
from jax.experimental.pallas import tpu as pltpu
from jax.sharding import PartitionSpec as P

QUERY_HEADS = 64
KEY_HEADS = 8
HEAD_DIM = 128
BEAM_COUNT = 16
STEPS = 3


EPS = 1e-06
NEG = -1e30
ROPE_BASE = 1000000.0


def rope_parts(positions, head_size):
    half = head_size // 2
    freqs = np.power(ROPE_BASE, -np.arange(half) * 2.0 / head_size)
    angle = positions.astype(jnp.float32)[:, None] * jnp.asarray(freqs, jnp.float32)[None, :]
    return (jnp.cos(angle), jnp.sin(angle))


def apply_rotation(value_rows, cosine_table, sine_table):
    half = value_rows.shape[-1] // 2
    first = value_rows[..., :half]
    second = value_rows[..., half:]
    cosine_table = cosine_table[:, None, :]
    sine_table = sine_table[:, None, :]
    return jnp.concatenate(
        [first * cosine_table - second * sine_table, second * cosine_table + first * sine_table],
        axis=-1,
    )


def local_by_rows(
    hidden,
    norm_gain,
    q_weight,
    q_bias,
    kv_weight,
    kv_bias,
    o_weight,
    prefix_key_cache,
    prefix_value_cache,
    prefix_index,
    prefix_lens,
    tail_key_cache,
    tail_value_cache,
    tail_lens,
    parents,
):
    devices = lax.axis_size("beam")
    me = lax.axis_index("beam")
    rows_per_chip = hidden.shape[1]
    width = hidden.shape[2]
    all_rows = rows_per_chip * devices
    prompt_batch = all_rows // BEAM_COUNT
    head_group = QUERY_HEADS // KEY_HEADS
    q_width = QUERY_HEADS * HEAD_DIM
    q_cols = q_weight.shape[1]
    kv_cols = kv_weight.shape[2]
    prefix_slice = prefix_key_cache.shape[1]
    tail_cache = tail_key_cache.shape[1]
    score_scale = 1.0 / math.sqrt(HEAD_DIM)
    row_ids = jnp.arange(all_rows, dtype=jnp.int32)
    prompt_of = row_ids // BEAM_COUNT
    first_row = me * rows_per_chip
    my_prompt = first_row // BEAM_COUNT
    slot_ids = first_row + jnp.arange(rows_per_chip, dtype=jnp.int32)
    mine = (jnp.arange(prompt_batch, dtype=jnp.int32) == my_prompt)[:, None, None, None]
    joint = jnp.concatenate([q_weight, kv_weight.reshape(width, 2 * kv_cols)], axis=1)
    joint_bias = jnp.concatenate([q_bias, kv_bias.reshape(2 * kv_cols)])
    slice_keys = jnp.take(prefix_key_cache, prefix_index, axis=0).reshape(
        prompt_batch, prefix_slice, KEY_HEADS, HEAD_DIM
    )
    slice_values = jnp.take(prefix_value_cache, prefix_index, axis=0).reshape(
        prompt_batch, prefix_slice, KEY_HEADS, HEAD_DIM
    )
    slab_ok = (me * prefix_slice + jnp.arange(prefix_slice, dtype=jnp.int32))[
        None, :
    ] < prefix_lens[:, None]
    slab_ok = slab_ok[:, None, None, None, :]
    tail_key_rows = tail_key_cache.reshape(rows_per_chip, tail_cache, KEY_HEADS, HEAD_DIM)
    tail_value_rows = tail_value_cache.reshape(rows_per_chip, tail_cache, KEY_HEADS, HEAD_DIM)
    own_lens = lax.dynamic_slice_in_dim(tail_lens, first_row, rows_per_chip, 0)
    tail_ok = jnp.arange(tail_cache, dtype=jnp.int32)[None, :] < own_lens[:, None]
    ancestors = row_ids
    makers = []
    fresh_keys = []
    current_values = []
    results = []
    for step in range(STEPS):
        chosen = parents[step]
        ancestors = ancestors[chosen]
        makers = [item[chosen] for item in makers] + [row_ids]
        value_rows = lax.all_gather(hidden[step], "beam", axis=0, tiled=True).astype(jnp.float32)
        normed = (
            value_rows
            * lax.rsqrt(jnp.mean(value_rows * value_rows, axis=-1, keepdims=True) + EPS)
            * norm_gain
        ).astype(jnp.bfloat16)
        projected = jnp.dot(normed, joint, preferred_element_type=jnp.float32) + joint_bias
        q_part = projected[:, :q_cols].astype(jnp.bfloat16)
        kv_part = projected[:, q_cols:].astype(jnp.bfloat16).reshape(all_rows, 2, kv_cols)
        positions = prefix_lens[prompt_of] + tail_lens[ancestors] + step
        cosine_table, sine_table = rope_parts(positions, HEAD_DIM)
        q_full, kv_full = (
            lax.all_gather(q_part[:, None, :], "beam", axis=2, tiled=True),
            lax.all_gather(kv_part, "beam", axis=2, tiled=True),
        )
        q_all = q_full[:, 0, :]
        owned_key_value = lax.dynamic_slice_in_dim(kv_full, first_row, rows_per_chip, 0)
        rotated_rows = apply_rotation(
            q_all.astype(jnp.float32).reshape(all_rows, QUERY_HEADS, HEAD_DIM),
            cosine_table,
            sine_table,
        ).astype(jnp.bfloat16)
        local_cosine = lax.dynamic_slice_in_dim(cosine_table, first_row, rows_per_chip, 0)
        local_sine = lax.dynamic_slice_in_dim(sine_table, first_row, rows_per_chip, 0)
        new_key = apply_rotation(
            owned_key_value[:, 0].astype(jnp.float32).reshape(rows_per_chip, KEY_HEADS, HEAD_DIM),
            local_cosine,
            local_sine,
        ).astype(jnp.bfloat16)
        fresh_keys.append(new_key)
        current_values.append(owned_key_value[:, 1].reshape(rows_per_chip, KEY_HEADS, HEAD_DIM))
        query_rows = rotated_rows.reshape(prompt_batch, BEAM_COUNT, KEY_HEADS, head_group, HEAD_DIM)
        pre_scores = (
            jnp.einsum(
                "pbkgd,pskd->pbkgs", query_rows, slice_keys, preferred_element_type=jnp.float32
            )
            * score_scale
        )
        pre_scores = jnp.where(slab_ok, pre_scores, NEG)
        local_q = lax.dynamic_index_in_dim(query_rows, my_prompt, 0, keepdims=False)
        local_anc = lax.dynamic_slice_in_dim(ancestors, my_prompt * BEAM_COUNT, BEAM_COUNT, 0)
        t_scores = (
            jnp.einsum(
                "bkgd,itkd->bkgit", local_q, tail_key_rows, preferred_element_type=jnp.float32
            )
            * score_scale
        )
        t_valid = (local_anc[:, None] == slot_ids[None, :])[:, None, None, :, None] & tail_ok[
            None, None, None, :, :
        ]
        t_scores = jnp.where(t_valid, t_scores, NEG)
        f_keys = jnp.stack(fresh_keys, 0)
        f_values = jnp.stack(current_values, 0)
        local_made = jnp.stack(
            [
                lax.dynamic_slice_in_dim(item, my_prompt * BEAM_COUNT, BEAM_COUNT, 0)
                for item in makers
            ],
            1,
        )
        f_valid = (local_made[:, :, None] == slot_ids[None, None, :])[:, None, None, :, :]
        f_scores = (
            jnp.einsum("bkgd,jikd->bkgji", local_q, f_keys, preferred_element_type=jnp.float32)
            * score_scale
        )
        f_scores = jnp.where(f_valid, f_scores, NEG)
        local_max = jnp.maximum(t_scores.max(axis=(3, 4)), f_scores.max(axis=(3, 4)))
        pre_max = pre_scores.max(-1)
        group_maximum = jnp.where(mine, jnp.maximum(pre_max, local_max[None]), pre_max)
        mine_max = lax.dynamic_index_in_dim(group_maximum, my_prompt, 0, keepdims=False)
        pre_w = jnp.where(slab_ok, jnp.exp(pre_scores - group_maximum[..., None]), 0.0)
        totals = pre_w.sum(-1)
        numer = jnp.einsum(
            "pbkgs,pskd->pbkgd",
            pre_w.astype(jnp.bfloat16),
            slice_values,
            preferred_element_type=jnp.float32,
        )
        t_w = jnp.where(t_valid, jnp.exp(t_scores - mine_max[..., None, None]), 0.0)
        f_w = jnp.where(f_valid, jnp.exp(f_scores - mine_max[..., None, None]), 0.0)
        local_total = t_w.sum(axis=(3, 4)) + f_w.sum(axis=(3, 4))
        local_num = jnp.einsum(
            "bkgit,itkd->bkgd",
            t_w.astype(jnp.bfloat16),
            tail_value_rows,
            preferred_element_type=jnp.float32,
        )
        local_num = local_num + jnp.einsum(
            "bkgji,jikd->bkgd",
            f_w.astype(jnp.bfloat16),
            f_values,
            preferred_element_type=jnp.float32,
        )
        totals = jnp.where(mine, totals + local_total[None], totals)
        numer = jnp.where(mine[..., None], numer + local_num[None], numer)
        sending = numer.astype(jnp.bfloat16).reshape(devices, rows_per_chip, q_width)
        parts = lax.all_to_all(sending, "beam", split_axis=0, concat_axis=0, tiled=True)
        maxima, sums = (
            lax.all_to_all(
                group_maximum.reshape(devices, rows_per_chip, QUERY_HEADS),
                "beam",
                split_axis=0,
                concat_axis=0,
                tiled=True,
            ),
            lax.all_to_all(
                totals.reshape(devices, rows_per_chip, QUERY_HEADS),
                "beam",
                split_axis=0,
                concat_axis=0,
                tiled=True,
            ),
        )
        top = maxima.max(0)
        factors = jnp.exp(maxima - top[None])
        denom = (factors * sums).sum(0)
        combined = jnp.einsum(
            "srh,srhd->rhd",
            factors,
            parts.reshape(devices, rows_per_chip, QUERY_HEADS, HEAD_DIM),
            preferred_element_type=jnp.float32,
        )
        attention = (
            (combined / denom[..., None]).reshape(rows_per_chip, q_width).astype(jnp.bfloat16)
        )
        out_cols = jnp.dot(
            lax.all_gather(attention, "beam", axis=0, tiled=True),
            o_weight,
            preferred_element_type=jnp.float32,
        )
        results.append(out_cols.astype(jnp.bfloat16))
    return jnp.stack(results, 0)


MESH = pl.DeviceIdType.MESH


def place():
    me = lax.axis_index("beam")
    return me, me // 4, me // 2 % 2, me % 2


def at(z, y, c):
    return (z * 2 + y) * 2 + c


def partners(z):
    return [z + 1 - 2 * (z % 2), (z + 2) % 4, 3 - z]


def line(z):
    near = z + 1 - 2 * (z % 2)
    return [(near, 3 - z), (2 - z // 2, near), (3 - 3 * (z // 2), near)]


def middle(z):
    return (z + 1) // 2 == 1


def greet(z, y, c):
    barrier = pltpu.get_barrier_semaphore()
    others = [at(w, y, c) for w in partners(z)] + [at(z, 1 - y, c), at(z, y, 1 - c)]
    for other in others:
        pl.semaphore_signal(barrier, inc=1, device_id={"beam": other}, device_id_type=MESH)
    pl.semaphore_wait(barrier, len(others))


class Gather:
    def __init__(self, x_ref, o_ref, send, recv):
        self.x_ref, self.o_ref, self.send, self.recv = x_ref, o_ref, send, recv
        self.me, self.z, self.y, self.c = place()
        self.sent = []

    def push(self, shard, target, src, only=None):
        copy = pltpu.make_async_remote_copy(
            src_ref=src,
            dst_ref=self.o_ref.at[shard],
            send_sem=self.send.at[len(self.sent)],
            recv_sem=self.recv.at[shard],
            device_id={"beam": target},
            device_id_type=MESH,
        )
        if only is None:
            copy.start()
        else:
            pl.when(only)(copy.start)
        self.sent.append((copy, only))

    def arrive(self, shard):
        pltpu.make_async_remote_copy(
            src_ref=self.o_ref.at[shard],
            dst_ref=self.o_ref.at[shard],
            send_sem=self.send.at[0],
            recv_sem=self.recv.at[shard],
            device_id={"beam": at(self.z, self.y, 1 - self.c)},
            device_id_type=MESH,
        ).wait_recv()

    def run(self, use):
        z, y, c = self.z, self.y, self.c
        over, core = at(z, 1 - y, c), at(z, y, 1 - c)
        hops = line(z)
        zs = [w for w, _ in hops]
        inner = middle(z)
        self.push(self.me, at(3 - z, y, c), self.x_ref, inner)
        self.push(self.me, at(zs[0], y, c), self.x_ref)
        self.push(self.me, over, self.x_ref)
        self.push(self.me, core, self.x_ref)
        use(self.me)
        for w, onward in hops:
            shard = at(w, y, c)
            self.arrive(shard)
            self.push(shard, at(onward, y, c), self.o_ref.at[shard], inner)
            self.push(shard, over, self.o_ref.at[shard])
            self.push(shard, core, self.o_ref.at[shard])
            use(shard)
        for w in [z] + zs:
            shard = at(w, 1 - y, c)
            self.arrive(shard)
            self.push(shard, core, self.o_ref.at[shard])
            use(shard)
        for w in [z] + zs:
            for v in (y, 1 - y):
                shard = at(w, v, 1 - c)
                self.arrive(shard)
                use(shard)
        for copy, only in self.sent:
            if only is None:
                copy.wait_send()
            else:
                pl.when(only)(copy.wait_send)


def gather_kernel(x_ref, o_ref, send, recv):
    me, z, y, c = place()
    greet(z, y, c)
    o_ref[me] = x_ref[...]
    Gather(x_ref, o_ref, send, recv).run(lambda shard: None)


def gather(x, devices, tag):
    vmem = pl.BlockSpec(memory_space=pltpu.VMEM)
    return pl.pallas_call(
        gather_kernel,
        out_shape=jax.ShapeDtypeStruct((devices,) + x.shape, x.dtype),
        in_specs=[vmem],
        out_specs=vmem,
        scratch_shapes=[pltpu.SemaphoreType.DMA((19,)), pltpu.SemaphoreType.DMA((16,))],
        compiler_params=pltpu.CompilerParams(
            collective_id=tag, has_side_effects=True, vmem_limit_bytes=32 * 2**20
        ),
    )(x)


def merge_kernel(
    heads, rows, num_ref, st_ref, ow_ref, out_ref,
    in1, st1, acc1, sacc1, in2, st2, acc2, sacc2, in3, st3, att, full, weight,
    send, recv, gsend, grecv, wsem,
):
    me, z, y, c = place()
    fetch = pltpu.make_async_copy(ow_ref, weight, wsem)
    fetch.start()
    greet(z, y, c)
    over, core = at(z, 1 - y, c), at(z, y, 1 - c)
    order = partners(z)[::-1] + [z]
    started = []

    def ship(src, ssrc, dst, sdst, target):
        slot = len(started)
        for copy_src, copy_dst, lane in ((src, dst, 0), (ssrc, sdst, 1)):
            pltpu.make_async_remote_copy(
                src_ref=copy_src, dst_ref=copy_dst, send_sem=send.at[slot, lane], recv_sem=recv.at[slot, lane],
                device_id={"beam": target}, device_id_type=MESH,
            ).start()
        started.append((src, ssrc, dst, sdst, target))

    def handle(slot, lane):
        src, ssrc, dst, sdst, target = started[slot]
        return pltpu.make_async_remote_copy(
            src_ref=(src, ssrc)[lane], dst_ref=(dst, sdst)[lane], send_sem=send.at[slot, lane],
            recv_sem=recv.at[slot, lane], device_id={"beam": target}, device_id_type=MESH,
        )

    def landed(slot):
        handle(slot, 0).wait_recv()
        handle(slot, 1).wait_recv()

    def weigh(stats):
        top = stats[0][:heads]
        for item in stats[1:]:
            top = jnp.maximum(top, item[:heads])
        scale = [jnp.exp(item[:heads] - top) for item in stats]
        total = scale[0] * stats[0][heads:]
        for e, item in zip(scale[1:], stats[1:]):
            total = total + e * item[heads:]
        return top, scale, total

    def flip(top_half, low_half):
        return jnp.transpose(jnp.concatenate([top_half, low_half], 0))

    def merge(a, sa, b, sb, dst, sdst):
        top, scale, total = weigh([sa[...], sb[...]])
        sdst[...] = jnp.concatenate([top, total], 0)
        e = flip(scale[0], scale[1])
        for h in range(heads):
            part = pl.ds(h * rows, rows)
            dst[part, :] = (
                a[part, :].astype(jnp.float32) * e[:rows, h : h + 1]
                + b[part, :].astype(jnp.float32) * e[:rows, heads + h : heads + h + 1]
            ).astype(jnp.bfloat16)

    for v, base in ((1 - y, 0), (y, 4)):
        for k, w in enumerate(order):
            chunk = at(w, v, 1 - c)
            ship(num_ref.at[chunk], st_ref.at[chunk], in1.at[base + k], st1.at[base + k], core)
    for k, w in enumerate(order):
        chunk = at(w, 1 - y, c)
        landed(k)
        merge(num_ref.at[chunk], st_ref.at[chunk], in1.at[k], st1.at[k], acc1.at[k], sacc1.at[k])
        ship(acc1.at[k], sacc1.at[k], in2.at[k], st2.at[k], over)
    for k, w in enumerate(order):
        chunk = at(w, y, c)
        landed(4 + k)
        merge(num_ref.at[chunk], st_ref.at[chunk], in1.at[4 + k], st1.at[4 + k], acc1.at[4 + k], sacc1.at[4 + k])
    for k, w in enumerate(order):
        landed(8 + k)
        merge(acc1.at[4 + k], sacc1.at[4 + k], in2.at[k], st2.at[k], acc2.at[k], sacc2.at[k])
        if k < 3:
            ship(acc2.at[k], sacc2.at[k], in3.at[k], st3.at[k], at(w, y, c))
    for k in range(3):
        landed(12 + k)
    stats = [sacc2[3]] + [st3[k] for k in range(3)]
    top, scale, total = weigh(stats)
    e01, e23 = flip(scale[0], scale[1]), flip(scale[2], scale[3])
    below = flip(total, total)
    for h in range(heads):
        part = pl.ds(h * rows, rows)
        value = acc2[3, part, :].astype(jnp.float32) * e01[:rows, h : h + 1]
        for k, table, lane in ((0, e01, heads + h), (1, e23, h), (2, e23, heads + h)):
            value = value + in3[k, part, :].astype(jnp.float32) * table[:rows, lane : lane + 1]
        att[:, h * HEAD_DIM : (h + 1) * HEAD_DIM] = (value / below[:rows, h : h + 1]).astype(jnp.bfloat16)
    full[me] = att[...]
    fetch.wait()
    depth = heads * HEAD_DIM
    total = [None]

    def use(shard):
        term = jnp.dot(
            full[shard], weight[pl.ds(shard * depth, depth), :], preferred_element_type=jnp.float32
        )
        total[0] = term if total[0] is None else total[0] + term

    Gather(att, full, gsend, grecv).run(use)
    out_ref[...] = total[0].astype(jnp.bfloat16)
    for slot in range(len(started)):
        handle(slot, 0).wait_send()
        handle(slot, 1).wait_send()


def merge_and_project(num, stats, o_weight, heads, rows, tag):
    devices = num.shape[0]
    vmem = pl.BlockSpec(memory_space=pltpu.VMEM)
    chunk = num.shape[1:]
    depth, cols = o_weight.shape
    bf = lambda k: pltpu.VMEM((k,) + chunk, jnp.bfloat16)
    fl = lambda k: pltpu.VMEM((k,) + stats.shape[1:], jnp.float32)
    return pl.pallas_call(
        lambda *refs: merge_kernel(heads, rows, *refs),
        out_shape=jax.ShapeDtypeStruct((rows, cols), jnp.bfloat16),
        in_specs=[vmem, vmem, pl.BlockSpec(memory_space=pl.ANY)],
        out_specs=vmem,
        scratch_shapes=[
            bf(8), fl(8), bf(8), fl(8), bf(4), fl(4), bf(4), fl(4), bf(3), fl(3),
            pltpu.VMEM((rows, heads * HEAD_DIM), jnp.bfloat16),
            pltpu.VMEM((devices, rows, heads * HEAD_DIM), jnp.bfloat16),
            pltpu.VMEM((depth, cols), jnp.bfloat16),
            pltpu.SemaphoreType.DMA((15, 2)),
            pltpu.SemaphoreType.DMA((15, 2)),
            pltpu.SemaphoreType.DMA((19,)),
            pltpu.SemaphoreType.DMA((16,)),
            pltpu.SemaphoreType.DMA,
        ],
        compiler_params=pltpu.CompilerParams(
            collective_id=tag, has_side_effects=True, vmem_limit_bytes=40 * 2**20
        ),
    )(num, stats, o_weight)


def attend_kernel(
    own, scale, x_ref, pk_ref, pv_ref, tk_ref, tv_ref, pok_ref, lok_ref, cs_ref, sn_ref,
    num_ref, st_ref, full, column, send, recv,
):
    me, z, y, c = place()
    greet(z, y, c)
    full[me] = x_ref[...]
    column[...] = jnp.zeros_like(column)
    over, core = at(z, 1 - y, c), at(z, y, 1 - c)
    heads = x_ref.shape[0] - 1
    rows = x_ref.shape[1]
    ppr = rows // 2
    tail = tk_ref.shape[0]
    my_prompt = me // 8
    group = 2 * heads

    def push(slot, shard, target, src):
        pltpu.make_async_remote_copy(
            src_ref=src, dst_ref=full.at[shard], send_sem=send.at[slot], recv_sem=recv.at[shard],
            device_id={"beam": target}, device_id_type=MESH,
        ).start()

    def arrive(shard):
        pltpu.make_async_remote_copy(
            src_ref=full.at[shard], dst_ref=full.at[shard], send_sem=send.at[0], recv_sem=recv.at[shard],
            device_id={"beam": core}, device_id_type=MESH,
        ).wait_recv()

    inner = middle(z)
    hops = line(z)

    @pl.when(inner)
    def _():
        push(15, me, at(3 - z, y, c), x_ref)

    push(1, me, at(hops[0][0], y, c), x_ref)
    push(0, me, over, x_ref)
    push(2, me, core, x_ref)
    for k, (w, onward) in enumerate(hops):
        shard = at(w, y, c)
        arrive(shard)

        @pl.when(inner)
        def _():
            push(16 + k, shard, at(onward, y, c), full.at[shard])

        push(5 + 2 * k, shard, over, full.at[shard])
        push(6 + 2 * k, shard, core, full.at[shard])

    lane = lax.broadcasted_iota(jnp.int32, (16, HEAD_DIM), 1)
    pick_row = lax.broadcasted_iota(jnp.int32, (16, rows), 0)
    pick_col = lax.broadcasted_iota(jnp.int32, (16, rows), 1)
    hot = jnp.where((pick_col == me * own + pick_row) & (pick_row < own), 1.0, 0.0).astype(jnp.bfloat16)
    wide = lax.broadcasted_iota(jnp.int32, (ppr, 128), 1)
    contract = (((1,), (1,)), ((), ()))

    def queries(k, prompt):
        start = pl.multiple_of(prompt * ppr, 16)
        return jnp.concatenate(
            [full[2 * k + g // heads, g % heads, pl.ds(start, ppr), :] for g in range(group)], 0
        )

    def write(k, prompt, num, top, total):
        start = pl.multiple_of(prompt * ppr, 16)
        num = num.astype(jnp.bfloat16)
        table = jnp.zeros((ppr, 128), jnp.float32)
        for g in range(group):
            part = slice(g * ppr, (g + 1) * ppr)
            place_at = pl.multiple_of(g % heads * rows + prompt * ppr, 16)
            num_ref[2 * k + g // heads, pl.ds(place_at, ppr), :] = num[part]
            base = g // heads * 2 * heads + g % heads
            table = jnp.where(wide == base, top[part], table)
            table = jnp.where(wide == base + heads, total[part], table)
        column[pl.ds(start, ppr), :] = table

    def one(i, carry):
        turn = i % 4
        odd, high = turn % 2, turn // 2
        w = z + odd * (1 - high) * (hops[0][0] - z) + (1 - odd) * high * (hops[1][0] - z) + odd * high * (hops[2][0] - z)
        v = (y + i // 4) % 2

        @pl.when(i < 4)
        def _():
            shard = at(w, 1 - y, c)
            arrive(shard)
            push(11 + i, shard, core, full.at[shard])

        arrive(at(w, v, 1 - c))
        k = w * 2 + v
        cols = pl.ds(pl.multiple_of(k * HEAD_DIM, HEAD_DIM), HEAD_DIM)
        lo = jnp.dot(hot, full[2 * k, heads], preferred_element_type=jnp.float32)
        hi = jnp.dot(hot, full[2 * k + 1, heads], preferred_element_type=jnp.float32)
        key = jnp.where(lane < HEAD_DIM // 2, lo, pltpu.roll(hi, HEAD_DIM // 2, 1))
        value = jnp.where(lane < HEAD_DIM // 2, pltpu.roll(lo, HEAD_DIM // 2, 1), hi)
        key = key * cs_ref[...] + pltpu.roll(key, HEAD_DIM // 2, 1) * sn_ref[...]
        blank = jnp.zeros((128 - 16, HEAD_DIM), jnp.bfloat16)
        key = jnp.concatenate([key.astype(jnp.bfloat16), blank], 0)
        value = jnp.concatenate([value.astype(jnp.bfloat16), blank], 0)

        def prefix(prompt, q):
            keys = pk_ref[prompt, :, cols]
            s = lax.dot_general(q, keys, contract, preferred_element_type=jnp.float32) * scale
            ok = pok_ref[prompt][:1] > 0.0
            return jnp.where(ok, s, NEG), ok

        q = queries(k, 1 - my_prompt)
        s, ok = prefix(1 - my_prompt, q)
        top = jnp.max(s, axis=1, keepdims=True)
        e = jnp.where(ok, jnp.exp(s - top), 0.0)
        num = jnp.dot(e.astype(jnp.bfloat16), pv_ref[1 - my_prompt, :, cols], preferred_element_type=jnp.float32)
        write(k, 1 - my_prompt, num, top, jnp.sum(e, axis=1, keepdims=True))

        q = queries(k, my_prompt)
        s, ok = prefix(my_prompt, q)
        ls = jnp.concatenate(
            [
                lax.dot_general(q, tk_ref[:, cols], contract, preferred_element_type=jnp.float32),
                lax.dot_general(q, key, contract, preferred_element_type=jnp.float32),
            ],
            1,
        )
        lok = jnp.concatenate([lok_ref[...]] * group, 0) > 0.0
        ls = jnp.where(lok, ls * scale, NEG)
        top = jnp.maximum(jnp.max(s, axis=1, keepdims=True), jnp.max(ls, axis=1, keepdims=True))
        e = jnp.where(ok, jnp.exp(s - top), 0.0)
        le = jnp.where(lok, jnp.exp(ls - top), 0.0)
        total = jnp.sum(e, axis=1, keepdims=True) + jnp.sum(le, axis=1, keepdims=True)
        le = le.astype(jnp.bfloat16)
        num = jnp.dot(e.astype(jnp.bfloat16), pv_ref[my_prompt, :, cols], preferred_element_type=jnp.float32)
        num = num + jnp.dot(le[:, :tail], tv_ref[:, cols], preferred_element_type=jnp.float32)
        num = num + jnp.dot(le[:, tail:], value, preferred_element_type=jnp.float32)
        write(k, my_prompt, num, top, total)

        flat = jnp.transpose(column[...])
        st_ref[2 * k] = flat[: 2 * heads]
        st_ref[2 * k + 1] = flat[2 * heads : 4 * heads]
        return carry

    lax.fori_loop(0, 8, one, 0)

    def sent(slot):
        pltpu.make_async_remote_copy(
            src_ref=x_ref, dst_ref=full.at[0], send_sem=send.at[slot], recv_sem=recv.at[0],
            device_id={"beam": core}, device_id_type=MESH,
        ).wait_send()

    for slot in [0, 1, 2] + list(range(5, 15)):
        sent(slot)

    @pl.when(inner)
    def _():
        for slot in range(15, 19):
            sent(slot)


def gather_and_attend(pieces, pk, pv, tk, tv, pok, lok, cs, sn, own, scale, devices, tag):
    vmem = pl.BlockSpec(memory_space=pltpu.VMEM)
    heads, rows = pieces.shape[0] - 1, pieces.shape[1]
    return pl.pallas_call(
        lambda *refs: attend_kernel(own, scale, *refs),
        out_shape=[
            jax.ShapeDtypeStruct((devices, heads * rows, HEAD_DIM), jnp.bfloat16),
            jax.ShapeDtypeStruct((devices, 2 * heads, 128), jnp.float32),
        ],
        in_specs=[vmem] * 9,
        out_specs=[vmem, vmem],
        scratch_shapes=[
            pltpu.VMEM((devices,) + pieces.shape, jnp.bfloat16),
            pltpu.VMEM((128, 128), jnp.float32),
            pltpu.SemaphoreType.DMA((19,)),
            pltpu.SemaphoreType.DMA((16,)),
        ],
        compiler_params=pltpu.CompilerParams(
            collective_id=tag, has_side_effects=True, vmem_limit_bytes=40 * 2**20
        ),
    )(pieces, pk, pv, tk, tv, pok, lok, cs, sn)


def lineage_tables(parents, prefix_lens, tail_lens, rows_per_chip, devices):
    all_rows = parents.shape[1]
    row_ids = jnp.arange(all_rows, dtype=jnp.int32)
    ancestors = row_ids
    makers = []
    anc_steps, pos_steps, maker_steps = [], [], []
    base = prefix_lens[row_ids // BEAM_COUNT]
    for step in range(STEPS):
        hot = parents[step][:, None] == row_ids[None, :]
        pick = lambda item: jnp.sum(jnp.where(hot, item[None, :], 0), axis=1)
        ancestors = pick(ancestors)
        makers = [pick(item) for item in makers] + [row_ids]
        lens = jnp.sum(jnp.where(ancestors[:, None] == row_ids[None, :], tail_lens[None, :], 0), axis=1)
        anc_steps.append(ancestors)
        pos_steps.append(base + lens + step)
        maker_steps.append(jnp.stack(makers + [jnp.full_like(row_ids, -1)] * (STEPS - 1 - step), 0))

    def order(table):
        lead = table.shape[1:-1]
        table = table.reshape((STEPS,) + lead + (devices, rows_per_chip))
        table = jnp.moveaxis(table, -2, 0)
        table = jnp.moveaxis(table, 1, -2)
        return jnp.moveaxis(table, 0, -3).reshape(lead + (STEPS * all_rows,))

    return order(jnp.stack(anc_steps, 0)), order(jnp.stack(pos_steps, 0)), order(jnp.stack(maker_steps, 0))


def local(
    hidden,
    norm_gain,
    q_weight,
    q_bias,
    kv_weight,
    kv_bias,
    o_weight,
    prefix_key_cache,
    prefix_value_cache,
    prefix_index,
    prefix_lens,
    tail_key_cache,
    tail_value_cache,
    tail_lens,
    parents,
):
    devices = lax.axis_size("beam")
    me = lax.axis_index("beam")
    rpc = hidden.shape[1]
    width = hidden.shape[2]
    if devices != 16 or 2 * kv_weight.shape[2] != HEAD_DIM or STEPS * rpc > 8 or prefix_index.shape[0] != 2:
        return local_by_rows(
            hidden, norm_gain, q_weight, q_bias, kv_weight, kv_bias, o_weight, prefix_key_cache,
            prefix_value_cache, prefix_index, prefix_lens, tail_key_cache, tail_value_cache, tail_lens, parents,
        )
    own = STEPS * rpc
    rows = own * devices
    prompts = prefix_index.shape[0]
    ppr = rows // prompts
    heads = QUERY_HEADS // devices
    group = QUERY_HEADS // KEY_HEADS
    q_cols = q_weight.shape[1]
    kv_cols = kv_weight.shape[2]
    slab = prefix_key_cache.shape[1]
    tail = tail_key_cache.shape[1]
    score_scale = 1.0 / math.sqrt(HEAD_DIM)
    my_prompt = me * rpc // BEAM_COUNT
    anc, pos, made = lineage_tables(parents, prefix_lens, tail_lens, rpc, devices)

    x = hidden.astype(jnp.float32)
    normed = (x * lax.rsqrt(jnp.mean(x * x, axis=-1, keepdims=True) + EPS) * norm_gain).astype(jnp.bfloat16)
    normed = jnp.pad(normed.reshape(own, width), ((0, 8 - own), (0, 0)))
    normed = gather(normed, devices, 0).reshape(devices * 8, width)
    real = lambda v: v.reshape(devices, 8, v.shape[1])[:, :own].reshape(rows, v.shape[1])
    q = (jnp.dot(normed, q_weight, preferred_element_type=jnp.float32) + q_bias).astype(jnp.bfloat16)
    kv = jnp.dot(normed, kv_weight.reshape(width, 2 * kv_cols), preferred_element_type=jnp.float32)
    kv = (kv + kv_bias.reshape(2 * kv_cols)).astype(jnp.bfloat16)
    q, kv = real(q), real(kv)
    cosine, sine = rope_parts(pos, HEAD_DIM)
    cosine2 = jnp.concatenate([cosine, cosine], 1)
    sine2 = jnp.concatenate([-sine, sine], 1)

    def rotate(v):
        v = v.astype(jnp.float32)
        return (v * cosine2 + jnp.roll(v, HEAD_DIM // 2, axis=-1) * sine2).astype(jnp.bfloat16)

    pieces = [rotate(q[:, h * HEAD_DIM : (h + 1) * HEAD_DIM]) for h in range(heads)] + [kv]
    first = me * rpc
    slot = first + jnp.arange(rpc, dtype=jnp.int32)
    lanc = lax.dynamic_slice_in_dim(anc, my_prompt * ppr, ppr, 0)
    lmade = lax.dynamic_slice_in_dim(made, my_prompt * ppr, ppr, 1)
    own_lens = lax.dynamic_slice_in_dim(tail_lens, first, rpc, 0)
    t_ok = (lanc[:, None] == slot[None, :])[:, :, None] & (
        jnp.arange(tail, dtype=jnp.int32)[None, None, :] < own_lens[None, :, None]
    )
    f_ok = lmade.T[:, :, None] == slot[None, None, :]
    lok = jnp.concatenate([t_ok.reshape(ppr, rpc * tail), f_ok.reshape(ppr, own)], 1).astype(jnp.float32)
    lok = jnp.pad(lok, ((0, 0), (0, 128 - own)))
    pok = (me * slab + jnp.arange(slab, dtype=jnp.int32))[None, :] < prefix_lens[:, None]
    pok = jnp.broadcast_to(pok.astype(jnp.float32)[:, None], (prompts, 8, slab))
    my_cos = jnp.pad(lax.dynamic_slice_in_dim(cosine2, me * own, own, 0), ((0, 16 - own), (0, 0)))
    my_sin = jnp.pad(lax.dynamic_slice_in_dim(sine2, me * own, own, 0), ((0, 16 - own), (0, 0)))
    num, stats = gather_and_attend(
        jnp.stack(pieces, 0),
        jnp.take(prefix_key_cache, prefix_index, axis=0, mode="clip"),
        jnp.take(prefix_value_cache, prefix_index, axis=0, mode="clip"),
        tail_key_cache.reshape(rpc * tail, -1),
        tail_value_cache.reshape(rpc * tail, -1),
        pok, lok, my_cos, my_sin, own, score_scale, devices, 1,
    )
    out = merge_and_project(num, stats, o_weight, heads, rows, 2)
    out = out.reshape(devices, STEPS, rpc, out.shape[1])
    return jnp.transpose(out, (1, 0, 2, 3)).reshape(STEPS, devices * rpc, out.shape[3])


def solution(mesh):
    return jax.shard_map(
        local,
        mesh=mesh,
        in_specs=(
            P(None, ("grp", "beam"), None),
            P(),
            P(None, "beam"),
            P("beam"),
            P(None, None, "beam"),
            P(None, "beam"),
            P(None, "beam"),
            P("grp", "beam", None),
            P("grp", "beam", None),
            P("grp"),
            P("grp"),
            P(("grp", "beam"), None, None),
            P(("grp", "beam"), None, None),
            P("grp"),
            P(None, "grp"),
        ),
        out_specs=P(None, "grp", "beam"),
        check_vma=False,
    )
```

```python
import math

import jax
import jax.numpy as jnp
import numpy as np
from jax import lax
from jax.experimental import pallas as pl
from jax.experimental.pallas import tpu as pltpu
from jax.sharding import PartitionSpec as P

QUERY_HEADS = 64
KEY_HEADS = 8
HEAD_DIM = 128
BEAM_COUNT = 16
STEPS = 3


EPS = 1e-06
NEG = -1e30
ROPE_BASE = 1000000.0


def rope_parts(positions, head_size):
    half = head_size // 2
    freqs = np.power(ROPE_BASE, -np.arange(half) * 2.0 / head_size)
    angle = positions.astype(jnp.float32)[:, None] * jnp.asarray(freqs, jnp.float32)[None, :]
    return (jnp.cos(angle), jnp.sin(angle))


def apply_rotation(value_rows, cosine_table, sine_table):
    half = value_rows.shape[-1] // 2
    first = value_rows[..., :half]
    second = value_rows[..., half:]
    cosine_table = cosine_table[:, None, :]
    sine_table = sine_table[:, None, :]
    return jnp.concatenate(
        [first * cosine_table - second * sine_table, second * cosine_table + first * sine_table],
        axis=-1,
    )


def local_by_rows(
    hidden,
    norm_gain,
    q_weight,
    q_bias,
    kv_weight,
    kv_bias,
    o_weight,
    prefix_key_cache,
    prefix_value_cache,
    prefix_index,
    prefix_lens,
    tail_key_cache,
    tail_value_cache,
    tail_lens,
    parents,
):
    devices = lax.axis_size("beam")
    me = lax.axis_index("beam")
    rows_per_chip = hidden.shape[1]
    width = hidden.shape[2]
    all_rows = rows_per_chip * devices
    prompt_batch = all_rows // BEAM_COUNT
    head_group = QUERY_HEADS // KEY_HEADS
    q_width = QUERY_HEADS * HEAD_DIM
    q_cols = q_weight.shape[1]
    kv_cols = kv_weight.shape[2]
    prefix_slice = prefix_key_cache.shape[1]
    tail_cache = tail_key_cache.shape[1]
    score_scale = 1.0 / math.sqrt(HEAD_DIM)
    row_ids = jnp.arange(all_rows, dtype=jnp.int32)
    prompt_of = row_ids // BEAM_COUNT
    first_row = me * rows_per_chip
    my_prompt = first_row // BEAM_COUNT
    slot_ids = first_row + jnp.arange(rows_per_chip, dtype=jnp.int32)
    mine = (jnp.arange(prompt_batch, dtype=jnp.int32) == my_prompt)[:, None, None, None]
    joint = jnp.concatenate([q_weight, kv_weight.reshape(width, 2 * kv_cols)], axis=1)
    joint_bias = jnp.concatenate([q_bias, kv_bias.reshape(2 * kv_cols)])
    slice_keys = jnp.take(prefix_key_cache, prefix_index, axis=0).reshape(
        prompt_batch, prefix_slice, KEY_HEADS, HEAD_DIM
    )
    slice_values = jnp.take(prefix_value_cache, prefix_index, axis=0).reshape(
        prompt_batch, prefix_slice, KEY_HEADS, HEAD_DIM
    )
    slab_ok = (me * prefix_slice + jnp.arange(prefix_slice, dtype=jnp.int32))[
        None, :
    ] < prefix_lens[:, None]
    slab_ok = slab_ok[:, None, None, None, :]
    tail_key_rows = tail_key_cache.reshape(rows_per_chip, tail_cache, KEY_HEADS, HEAD_DIM)
    tail_value_rows = tail_value_cache.reshape(rows_per_chip, tail_cache, KEY_HEADS, HEAD_DIM)
    own_lens = lax.dynamic_slice_in_dim(tail_lens, first_row, rows_per_chip, 0)
    tail_ok = jnp.arange(tail_cache, dtype=jnp.int32)[None, :] < own_lens[:, None]
    ancestors = row_ids
    makers = []
    fresh_keys = []
    current_values = []
    results = []
    for step in range(STEPS):
        chosen = parents[step]
        ancestors = ancestors[chosen]
        makers = [item[chosen] for item in makers] + [row_ids]
        value_rows = lax.all_gather(hidden[step], "beam", axis=0, tiled=True).astype(jnp.float32)
        normed = (
            value_rows
            * lax.rsqrt(jnp.mean(value_rows * value_rows, axis=-1, keepdims=True) + EPS)
            * norm_gain
        ).astype(jnp.bfloat16)
        projected = jnp.dot(normed, joint, preferred_element_type=jnp.float32) + joint_bias
        q_part = projected[:, :q_cols].astype(jnp.bfloat16)
        kv_part = projected[:, q_cols:].astype(jnp.bfloat16).reshape(all_rows, 2, kv_cols)
        positions = prefix_lens[prompt_of] + tail_lens[ancestors] + step
        cosine_table, sine_table = rope_parts(positions, HEAD_DIM)
        q_full, kv_full = (
            lax.all_gather(q_part[:, None, :], "beam", axis=2, tiled=True),
            lax.all_gather(kv_part, "beam", axis=2, tiled=True),
        )
        q_all = q_full[:, 0, :]
        owned_key_value = lax.dynamic_slice_in_dim(kv_full, first_row, rows_per_chip, 0)
        rotated_rows = apply_rotation(
            q_all.astype(jnp.float32).reshape(all_rows, QUERY_HEADS, HEAD_DIM),
            cosine_table,
            sine_table,
        ).astype(jnp.bfloat16)
        local_cosine = lax.dynamic_slice_in_dim(cosine_table, first_row, rows_per_chip, 0)
        local_sine = lax.dynamic_slice_in_dim(sine_table, first_row, rows_per_chip, 0)
        new_key = apply_rotation(
            owned_key_value[:, 0].astype(jnp.float32).reshape(rows_per_chip, KEY_HEADS, HEAD_DIM),
            local_cosine,
            local_sine,
        ).astype(jnp.bfloat16)
        fresh_keys.append(new_key)
        current_values.append(owned_key_value[:, 1].reshape(rows_per_chip, KEY_HEADS, HEAD_DIM))
        query_rows = rotated_rows.reshape(prompt_batch, BEAM_COUNT, KEY_HEADS, head_group, HEAD_DIM)
        pre_scores = (
            jnp.einsum(
                "pbkgd,pskd->pbkgs", query_rows, slice_keys, preferred_element_type=jnp.float32
            )
            * score_scale
        )
        pre_scores = jnp.where(slab_ok, pre_scores, NEG)
        local_q = lax.dynamic_index_in_dim(query_rows, my_prompt, 0, keepdims=False)
        local_anc = lax.dynamic_slice_in_dim(ancestors, my_prompt * BEAM_COUNT, BEAM_COUNT, 0)
        t_scores = (
            jnp.einsum(
                "bkgd,itkd->bkgit", local_q, tail_key_rows, preferred_element_type=jnp.float32
            )
            * score_scale
        )
        t_valid = (local_anc[:, None] == slot_ids[None, :])[:, None, None, :, None] & tail_ok[
            None, None, None, :, :
        ]
        t_scores = jnp.where(t_valid, t_scores, NEG)
        f_keys = jnp.stack(fresh_keys, 0)
        f_values = jnp.stack(current_values, 0)
        local_made = jnp.stack(
            [
                lax.dynamic_slice_in_dim(item, my_prompt * BEAM_COUNT, BEAM_COUNT, 0)
                for item in makers
            ],
            1,
        )
        f_valid = (local_made[:, :, None] == slot_ids[None, None, :])[:, None, None, :, :]
        f_scores = (
            jnp.einsum("bkgd,jikd->bkgji", local_q, f_keys, preferred_element_type=jnp.float32)
            * score_scale
        )
        f_scores = jnp.where(f_valid, f_scores, NEG)
        local_max = jnp.maximum(t_scores.max(axis=(3, 4)), f_scores.max(axis=(3, 4)))
        pre_max = pre_scores.max(-1)
        group_maximum = jnp.where(mine, jnp.maximum(pre_max, local_max[None]), pre_max)
        mine_max = lax.dynamic_index_in_dim(group_maximum, my_prompt, 0, keepdims=False)
        pre_w = jnp.where(slab_ok, jnp.exp(pre_scores - group_maximum[..., None]), 0.0)
        totals = pre_w.sum(-1)
        numer = jnp.einsum(
            "pbkgs,pskd->pbkgd",
            pre_w.astype(jnp.bfloat16),
            slice_values,
            preferred_element_type=jnp.float32,
        )
        t_w = jnp.where(t_valid, jnp.exp(t_scores - mine_max[..., None, None]), 0.0)
        f_w = jnp.where(f_valid, jnp.exp(f_scores - mine_max[..., None, None]), 0.0)
        local_total = t_w.sum(axis=(3, 4)) + f_w.sum(axis=(3, 4))
        local_num = jnp.einsum(
            "bkgit,itkd->bkgd",
            t_w.astype(jnp.bfloat16),
            tail_value_rows,
            preferred_element_type=jnp.float32,
        )
        local_num = local_num + jnp.einsum(
            "bkgji,jikd->bkgd",
            f_w.astype(jnp.bfloat16),
            f_values,
            preferred_element_type=jnp.float32,
        )
        totals = jnp.where(mine, totals + local_total[None], totals)
        numer = jnp.where(mine[..., None], numer + local_num[None], numer)
        sending = numer.astype(jnp.bfloat16).reshape(devices, rows_per_chip, q_width)
        parts = lax.all_to_all(sending, "beam", split_axis=0, concat_axis=0, tiled=True)
        maxima, sums = (
            lax.all_to_all(
                group_maximum.reshape(devices, rows_per_chip, QUERY_HEADS),
                "beam",
                split_axis=0,
                concat_axis=0,
                tiled=True,
            ),
            lax.all_to_all(
                totals.reshape(devices, rows_per_chip, QUERY_HEADS),
                "beam",
                split_axis=0,
                concat_axis=0,
                tiled=True,
            ),
        )
        top = maxima.max(0)
        factors = jnp.exp(maxima - top[None])
        denom = (factors * sums).sum(0)
        combined = jnp.einsum(
            "srh,srhd->rhd",
            factors,
            parts.reshape(devices, rows_per_chip, QUERY_HEADS, HEAD_DIM),
            preferred_element_type=jnp.float32,
        )
        attention = (
            (combined / denom[..., None]).reshape(rows_per_chip, q_width).astype(jnp.bfloat16)
        )
        out_cols = jnp.dot(
            lax.all_gather(attention, "beam", axis=0, tiled=True),
            o_weight,
            preferred_element_type=jnp.float32,
        )
        results.append(out_cols.astype(jnp.bfloat16))
    return jnp.stack(results, 0)


MESH = pl.DeviceIdType.MESH


def place():
    me = lax.axis_index("beam")
    return me, me // 4, me // 2 % 2, me % 2


def at(z, y, c):
    return (z * 2 + y) * 2 + c


def partners(z):
    return [z + 1 - 2 * (z % 2), (z + 2) % 4, 3 - z]


def line(z):
    near = z + 1 - 2 * (z % 2)
    return [(near, 3 - z), (2 - z // 2, near), (3 - 3 * (z // 2), near)]


def middle(z):
    return (z + 1) // 2 == 1


def greet(z, y, c):
    barrier = pltpu.get_barrier_semaphore()
    others = [at(w, y, c) for w in partners(z)] + [at(z, 1 - y, c), at(z, y, 1 - c)]
    for other in others:
        pl.semaphore_signal(barrier, inc=1, device_id={"beam": other}, device_id_type=MESH)
    pl.semaphore_wait(barrier, len(others))


class Gather:
    def __init__(self, x_ref, o_ref, send, recv):
        self.x_ref, self.o_ref, self.send, self.recv = x_ref, o_ref, send, recv
        self.me, self.z, self.y, self.c = place()
        self.sent = []

    def push(self, shard, target, src, only=None):
        copy = pltpu.make_async_remote_copy(
            src_ref=src,
            dst_ref=self.o_ref.at[shard],
            send_sem=self.send.at[len(self.sent)],
            recv_sem=self.recv.at[shard],
            device_id={"beam": target},
            device_id_type=MESH,
        )
        if only is None:
            copy.start()
        else:
            pl.when(only)(copy.start)
        self.sent.append((copy, only))

    def arrive(self, shard):
        pltpu.make_async_remote_copy(
            src_ref=self.o_ref.at[shard],
            dst_ref=self.o_ref.at[shard],
            send_sem=self.send.at[0],
            recv_sem=self.recv.at[shard],
            device_id={"beam": at(self.z, self.y, 1 - self.c)},
            device_id_type=MESH,
        ).wait_recv()

    def run(self, use):
        z, y, c = self.z, self.y, self.c
        over, core = at(z, 1 - y, c), at(z, y, 1 - c)
        hops = line(z)
        zs = [w for w, _ in hops]
        inner = middle(z)
        self.push(self.me, at(3 - z, y, c), self.x_ref, inner)
        self.push(self.me, at(zs[0], y, c), self.x_ref)
        self.push(self.me, over, self.x_ref)
        self.push(self.me, core, self.x_ref)
        use(self.me)
        for w, onward in hops:
            shard = at(w, y, c)
            self.arrive(shard)
            self.push(shard, at(onward, y, c), self.o_ref.at[shard], inner)
            self.push(shard, over, self.o_ref.at[shard])
            self.push(shard, core, self.o_ref.at[shard])
            use(shard)
        for w in [z] + zs:
            shard = at(w, 1 - y, c)
            self.arrive(shard)
            self.push(shard, core, self.o_ref.at[shard])
            use(shard)
        for w in [z] + zs:
            for v in (y, 1 - y):
                shard = at(w, v, 1 - c)
                self.arrive(shard)
                use(shard)
        for copy, only in self.sent:
            if only is None:
                copy.wait_send()
            else:
                pl.when(only)(copy.wait_send)


def gather_kernel(x_ref, o_ref, send, recv):
    me, z, y, c = place()
    greet(z, y, c)
    o_ref[me] = x_ref[...]
    Gather(x_ref, o_ref, send, recv).run(lambda shard: None)


def gather(x, devices, tag):
    vmem = pl.BlockSpec(memory_space=pltpu.VMEM)
    return pl.pallas_call(
        gather_kernel,
        out_shape=jax.ShapeDtypeStruct((devices,) + x.shape, x.dtype),
        in_specs=[vmem],
        out_specs=vmem,
        scratch_shapes=[pltpu.SemaphoreType.DMA((19,)), pltpu.SemaphoreType.DMA((16,))],
        compiler_params=pltpu.CompilerParams(
            collective_id=tag, has_side_effects=True, vmem_limit_bytes=32 * 2**20
        ),
    )(x)


def merge_kernel(
    heads, rows, num_ref, st_ref, ow_ref, out_ref,
    in1, st1, acc1, sacc1, in2, st2, acc2, sacc2, in3, st3, att, full, weight,
    send, recv, gsend, grecv, wsem,
):
    me, z, y, c = place()
    fetch = pltpu.make_async_copy(ow_ref, weight, wsem)
    fetch.start()
    greet(z, y, c)
    over, core = at(z, 1 - y, c), at(z, y, 1 - c)
    order = partners(z)[::-1] + [z]
    started = []

    def ship(src, ssrc, dst, sdst, target):
        slot = len(started)
        for copy_src, copy_dst, lane in ((src, dst, 0), (ssrc, sdst, 1)):
            pltpu.make_async_remote_copy(
                src_ref=copy_src, dst_ref=copy_dst, send_sem=send.at[slot, lane], recv_sem=recv.at[slot, lane],
                device_id={"beam": target}, device_id_type=MESH,
            ).start()
        started.append((src, ssrc, dst, sdst, target))

    def handle(slot, lane):
        src, ssrc, dst, sdst, target = started[slot]
        return pltpu.make_async_remote_copy(
            src_ref=(src, ssrc)[lane], dst_ref=(dst, sdst)[lane], send_sem=send.at[slot, lane],
            recv_sem=recv.at[slot, lane], device_id={"beam": target}, device_id_type=MESH,
        )

    def landed(slot):
        handle(slot, 0).wait_recv()
        handle(slot, 1).wait_recv()

    def weigh(stats):
        top = stats[0][:heads]
        for item in stats[1:]:
            top = jnp.maximum(top, item[:heads])
        scale = [jnp.exp(item[:heads] - top) for item in stats]
        total = scale[0] * stats[0][heads:]
        for e, item in zip(scale[1:], stats[1:]):
            total = total + e * item[heads:]
        return top, scale, total

    def flip(top_half, low_half):
        return jnp.transpose(jnp.concatenate([top_half, low_half], 0))

    def merge(a, sa, b, sb, dst, sdst):
        top, scale, total = weigh([sa[...], sb[...]])
        sdst[...] = jnp.concatenate([top, total], 0)
        e = flip(scale[0], scale[1])
        for h in range(heads):
            part = pl.ds(h * rows, rows)
            dst[part, :] = (
                a[part, :].astype(jnp.float32) * e[:rows, h : h + 1]
                + b[part, :].astype(jnp.float32) * e[:rows, heads + h : heads + h + 1]
            ).astype(jnp.bfloat16)

    for v, base in ((1 - y, 0), (y, 4)):
        for k, w in enumerate(order):
            chunk = at(w, v, 1 - c)
            ship(num_ref.at[chunk], st_ref.at[chunk], in1.at[base + k], st1.at[base + k], core)
    for k, w in enumerate(order):
        chunk = at(w, 1 - y, c)
        landed(k)
        merge(num_ref.at[chunk], st_ref.at[chunk], in1.at[k], st1.at[k], acc1.at[k], sacc1.at[k])
        ship(acc1.at[k], sacc1.at[k], in2.at[k], st2.at[k], over)
    for k, w in enumerate(order):
        chunk = at(w, y, c)
        landed(4 + k)
        merge(num_ref.at[chunk], st_ref.at[chunk], in1.at[4 + k], st1.at[4 + k], acc1.at[4 + k], sacc1.at[4 + k])
    for k, w in enumerate(order):
        landed(8 + k)
        merge(acc1.at[4 + k], sacc1.at[4 + k], in2.at[k], st2.at[k], acc2.at[k], sacc2.at[k])
        if k < 3:
            ship(acc2.at[k], sacc2.at[k], in3.at[k], st3.at[k], at(w, y, c))
    for k in range(3):
        landed(12 + k)
    stats = [sacc2[3]] + [st3[k] for k in range(3)]
    top, scale, total = weigh(stats)
    e01, e23 = flip(scale[0], scale[1]), flip(scale[2], scale[3])
    below = flip(total, total)
    for h in range(heads):
        part = pl.ds(h * rows, rows)
        value = acc2[3, part, :].astype(jnp.float32) * e01[:rows, h : h + 1]
        for k, table, lane in ((0, e01, heads + h), (1, e23, h), (2, e23, heads + h)):
            value = value + in3[k, part, :].astype(jnp.float32) * table[:rows, lane : lane + 1]
        att[:, h * HEAD_DIM : (h + 1) * HEAD_DIM] = (value / below[:rows, h : h + 1]).astype(jnp.bfloat16)
    full[me] = att[...]
    fetch.wait()
    depth = heads * HEAD_DIM
    total = [None]

    def use(shard):
        term = jnp.dot(
            full[shard], weight[pl.ds(shard * depth, depth), :], preferred_element_type=jnp.float32
        )
        total[0] = term if total[0] is None else total[0] + term

    Gather(att, full, gsend, grecv).run(use)
    out_ref[...] = total[0].astype(jnp.bfloat16)
    for slot in range(len(started)):
        handle(slot, 0).wait_send()
        handle(slot, 1).wait_send()


def merge_and_project(num, stats, o_weight, heads, rows, tag):
    devices = num.shape[0]
    vmem = pl.BlockSpec(memory_space=pltpu.VMEM)
    chunk = num.shape[1:]
    depth, cols = o_weight.shape
    bf = lambda k: pltpu.VMEM((k,) + chunk, jnp.bfloat16)
    fl = lambda k: pltpu.VMEM((k,) + stats.shape[1:], jnp.float32)
    return pl.pallas_call(
        lambda *refs: merge_kernel(heads, rows, *refs),
        out_shape=jax.ShapeDtypeStruct((rows, cols), jnp.bfloat16),
        in_specs=[vmem, vmem, pl.BlockSpec(memory_space=pltpu.HBM)],
        out_specs=vmem,
        scratch_shapes=[
            bf(8), fl(8), bf(8), fl(8), bf(4), fl(4), bf(4), fl(4), bf(3), fl(3),
            pltpu.VMEM((rows, heads * HEAD_DIM), jnp.bfloat16),
            pltpu.VMEM((devices, rows, heads * HEAD_DIM), jnp.bfloat16),
            pltpu.VMEM((depth, cols), jnp.bfloat16),
            pltpu.SemaphoreType.DMA((15, 2)),
            pltpu.SemaphoreType.DMA((15, 2)),
            pltpu.SemaphoreType.DMA((19,)),
            pltpu.SemaphoreType.DMA((16,)),
            pltpu.SemaphoreType.DMA,
        ],
        compiler_params=pltpu.CompilerParams(
            collective_id=tag, has_side_effects=True, vmem_limit_bytes=40 * 2**20
        ),
    )(num, stats, o_weight)


def attend_kernel(
    own, scale, x_ref, oh_ref, pk_ref, pv_ref, tk_ref, tv_ref, pok_ref, lok_ref, cs_ref, sn_ref,
    num_ref, st_ref, full, column, send, recv,
):
    me, z, y, c = place()
    greet(z, y, c)
    full[me] = x_ref[...]
    column[...] = jnp.zeros_like(column)
    over, core = at(z, 1 - y, c), at(z, y, 1 - c)
    heads = x_ref.shape[0] - 1
    rows = x_ref.shape[1]
    ppr = rows // 2
    tail = tk_ref.shape[0]
    my_prompt = me // 8
    group = 2 * heads

    def push(slot, shard, target, src):
        pltpu.make_async_remote_copy(
            src_ref=src, dst_ref=full.at[shard], send_sem=send.at[slot], recv_sem=recv.at[shard],
            device_id={"beam": target}, device_id_type=MESH,
        ).start()

    def arrive(shard):
        pltpu.make_async_remote_copy(
            src_ref=full.at[shard], dst_ref=full.at[shard], send_sem=send.at[0], recv_sem=recv.at[shard],
            device_id={"beam": core}, device_id_type=MESH,
        ).wait_recv()

    inner = middle(z)
    hops = line(z)

    @pl.when(inner)
    def _():
        push(15, me, at(3 - z, y, c), x_ref)

    push(1, me, at(hops[0][0], y, c), x_ref)
    push(0, me, over, x_ref)
    push(2, me, core, x_ref)
    for k, (w, onward) in enumerate(hops):
        shard = at(w, y, c)
        arrive(shard)

        @pl.when(inner)
        def _():
            push(16 + k, shard, at(onward, y, c), full.at[shard])

        push(5 + 2 * k, shard, over, full.at[shard])
        push(6 + 2 * k, shard, core, full.at[shard])

    lane = lax.broadcasted_iota(jnp.int32, (16, HEAD_DIM), 1)
    pick_row = lax.broadcasted_iota(jnp.int32, (16, rows), 0)
    pick_col = lax.broadcasted_iota(jnp.int32, (16, rows), 1)
    hot = jnp.where((pick_col == me * own + pick_row) & (pick_row < own), 1.0, 0.0).astype(jnp.bfloat16)
    wide = lax.broadcasted_iota(jnp.int32, (ppr, 128), 1)
    contract = (((1,), (1,)), ((), ()))

    def queries(k, prompt):
        start = pl.multiple_of(prompt * ppr, 16)
        return jnp.concatenate(
            [full[2 * k + g // heads, g % heads, pl.ds(start, ppr), :] for g in range(group)], 0
        )

    def write(k, prompt, num, top, total):
        start = pl.multiple_of(prompt * ppr, 16)
        num = num.astype(jnp.bfloat16)
        table = jnp.zeros((ppr, 128), jnp.float32)
        for g in range(group):
            part = slice(g * ppr, (g + 1) * ppr)
            place_at = pl.multiple_of(g % heads * rows + prompt * ppr, 16)
            num_ref[2 * k + g // heads, pl.ds(place_at, ppr), :] = num[part]
            base = g // heads * 2 * heads + g % heads
            table = jnp.where(wide == base, top[part], table)
            table = jnp.where(wide == base + heads, total[part], table)
        column[pl.ds(start, ppr), :] = table

    def one(i, carry):
        turn = i % 4
        odd, high = turn % 2, turn // 2
        w = z + odd * (1 - high) * (hops[0][0] - z) + (1 - odd) * high * (hops[1][0] - z) + odd * high * (hops[2][0] - z)
        v = (y + i // 4) % 2

        @pl.when(i < 4)
        def _():
            shard = at(w, 1 - y, c)
            arrive(shard)
            push(11 + i, shard, core, full.at[shard])

        arrive(at(w, v, 1 - c))
        k = w * 2 + v
        cols = pl.ds(pl.multiple_of(k * HEAD_DIM, HEAD_DIM), HEAD_DIM)
        lo = jnp.dot(hot, full[2 * k, heads], preferred_element_type=jnp.float32)
        hi = jnp.dot(hot, full[2 * k + 1, heads], preferred_element_type=jnp.float32)
        key = jnp.where(lane < HEAD_DIM // 2, lo, pltpu.roll(hi, HEAD_DIM // 2, 1))
        value = jnp.where(lane < HEAD_DIM // 2, pltpu.roll(lo, HEAD_DIM // 2, 1), hi)
        key = key * cs_ref[...] + pltpu.roll(key, HEAD_DIM // 2, 1) * sn_ref[...]
        blank = jnp.zeros((128 - 16, HEAD_DIM), jnp.bfloat16)
        key = jnp.concatenate([key.astype(jnp.bfloat16), blank], 0)
        value = jnp.concatenate([value.astype(jnp.bfloat16), blank], 0)

        def chosen(ref, prompt):
            entry = ref[0, :, cols].astype(jnp.float32) * oh_ref[prompt, 0][:1]
            for j in range(1, ref.shape[0]):
                entry = entry + ref[j, :, cols].astype(jnp.float32) * oh_ref[prompt, j][:1]
            return entry.astype(jnp.bfloat16)

        def prefix(prompt, q):
            keys = chosen(pk_ref, prompt)
            s = lax.dot_general(q, keys, contract, preferred_element_type=jnp.float32) * scale
            ok = pok_ref[prompt][:1] > 0.0
            return jnp.where(ok, s, NEG), ok

        q = queries(k, 1 - my_prompt)
        s, ok = prefix(1 - my_prompt, q)
        top = jnp.max(s, axis=1, keepdims=True)
        e = jnp.where(ok, jnp.exp(s - top), 0.0)
        num = jnp.dot(e.astype(jnp.bfloat16), chosen(pv_ref, 1 - my_prompt), preferred_element_type=jnp.float32)
        write(k, 1 - my_prompt, num, top, jnp.sum(e, axis=1, keepdims=True))

        q = queries(k, my_prompt)
        s, ok = prefix(my_prompt, q)
        ls = jnp.concatenate(
            [
                lax.dot_general(q, tk_ref[:, cols], contract, preferred_element_type=jnp.float32),
                lax.dot_general(q, key, contract, preferred_element_type=jnp.float32),
            ],
            1,
        )
        lok = jnp.concatenate([lok_ref[...]] * group, 0) > 0.0
        ls = jnp.where(lok, ls * scale, NEG)
        top = jnp.maximum(jnp.max(s, axis=1, keepdims=True), jnp.max(ls, axis=1, keepdims=True))
        e = jnp.where(ok, jnp.exp(s - top), 0.0)
        le = jnp.where(lok, jnp.exp(ls - top), 0.0)
        total = jnp.sum(e, axis=1, keepdims=True) + jnp.sum(le, axis=1, keepdims=True)
        le = le.astype(jnp.bfloat16)
        num = jnp.dot(e.astype(jnp.bfloat16), chosen(pv_ref, my_prompt), preferred_element_type=jnp.float32)
        num = num + jnp.dot(le[:, :tail], tv_ref[:, cols], preferred_element_type=jnp.float32)
        num = num + jnp.dot(le[:, tail:], value, preferred_element_type=jnp.float32)
        write(k, my_prompt, num, top, total)

        flat = jnp.transpose(column[...])
        st_ref[2 * k] = flat[: 2 * heads]
        st_ref[2 * k + 1] = flat[2 * heads : 4 * heads]
        return carry

    lax.fori_loop(0, 8, one, 0)

    def sent(slot):
        pltpu.make_async_remote_copy(
            src_ref=x_ref, dst_ref=full.at[0], send_sem=send.at[slot], recv_sem=recv.at[0],
            device_id={"beam": core}, device_id_type=MESH,
        ).wait_send()

    for slot in [0, 1, 2] + list(range(5, 15)):
        sent(slot)

    @pl.when(inner)
    def _():
        for slot in range(15, 19):
            sent(slot)


def gather_and_attend(pieces, oh, pk, pv, tk, tv, pok, lok, cs, sn, own, scale, devices, tag):
    vmem = pl.BlockSpec(memory_space=pltpu.VMEM)
    heads, rows = pieces.shape[0] - 1, pieces.shape[1]
    return pl.pallas_call(
        lambda *refs: attend_kernel(own, scale, *refs),
        out_shape=[
            jax.ShapeDtypeStruct((devices, heads * rows, HEAD_DIM), jnp.bfloat16),
            jax.ShapeDtypeStruct((devices, 2 * heads, 128), jnp.float32),
        ],
        in_specs=[vmem] * 10,
        out_specs=[vmem, vmem],
        scratch_shapes=[
            pltpu.VMEM((devices,) + pieces.shape, jnp.bfloat16),
            pltpu.VMEM((128, 128), jnp.float32),
            pltpu.SemaphoreType.DMA((19,)),
            pltpu.SemaphoreType.DMA((16,)),
        ],
        compiler_params=pltpu.CompilerParams(
            collective_id=tag, has_side_effects=True, vmem_limit_bytes=40 * 2**20
        ),
    )(pieces, oh, pk, pv, tk, tv, pok, lok, cs, sn)


def lineage_tables(parents, prefix_lens, tail_lens, rows_per_chip, devices):
    all_rows = parents.shape[1]
    row_ids = jnp.arange(all_rows, dtype=jnp.int32)
    ancestors = row_ids
    makers = []
    anc_steps, pos_steps, maker_steps = [], [], []
    base = prefix_lens[row_ids // BEAM_COUNT]
    for step in range(STEPS):
        hot = parents[step][:, None] == row_ids[None, :]
        pick = lambda item: jnp.sum(jnp.where(hot, item[None, :], 0), axis=1)
        ancestors = pick(ancestors)
        makers = [pick(item) for item in makers] + [row_ids]
        lens = jnp.sum(jnp.where(ancestors[:, None] == row_ids[None, :], tail_lens[None, :], 0), axis=1)
        anc_steps.append(ancestors)
        pos_steps.append(base + lens + step)
        maker_steps.append(jnp.stack(makers + [jnp.full_like(row_ids, -1)] * (STEPS - 1 - step), 0))

    def order(table):
        lead = table.shape[1:-1]
        table = table.reshape((STEPS,) + lead + (devices, rows_per_chip))
        table = jnp.moveaxis(table, -2, 0)
        table = jnp.moveaxis(table, 1, -2)
        return jnp.moveaxis(table, 0, -3).reshape(lead + (STEPS * all_rows,))

    return order(jnp.stack(anc_steps, 0)), order(jnp.stack(pos_steps, 0)), order(jnp.stack(maker_steps, 0))


def local(
    hidden,
    norm_gain,
    q_weight,
    q_bias,
    kv_weight,
    kv_bias,
    o_weight,
    prefix_key_cache,
    prefix_value_cache,
    prefix_index,
    prefix_lens,
    tail_key_cache,
    tail_value_cache,
    tail_lens,
    parents,
):
    devices = lax.axis_size("beam")
    me = lax.axis_index("beam")
    rpc = hidden.shape[1]
    width = hidden.shape[2]
    if devices != 16 or 2 * kv_weight.shape[2] != HEAD_DIM or STEPS * rpc > 8 or prefix_index.shape[0] != 2:
        return local_by_rows(
            hidden, norm_gain, q_weight, q_bias, kv_weight, kv_bias, o_weight, prefix_key_cache,
            prefix_value_cache, prefix_index, prefix_lens, tail_key_cache, tail_value_cache, tail_lens, parents,
        )
    own = STEPS * rpc
    rows = own * devices
    prompts = prefix_index.shape[0]
    ppr = rows // prompts
    heads = QUERY_HEADS // devices
    group = QUERY_HEADS // KEY_HEADS
    q_cols = q_weight.shape[1]
    kv_cols = kv_weight.shape[2]
    slab = prefix_key_cache.shape[1]
    tail = tail_key_cache.shape[1]
    score_scale = 1.0 / math.sqrt(HEAD_DIM)
    my_prompt = me * rpc // BEAM_COUNT
    anc, pos, made = lineage_tables(parents, prefix_lens, tail_lens, rpc, devices)

    x = hidden.astype(jnp.float32)
    normed = (x * lax.rsqrt(jnp.mean(x * x, axis=-1, keepdims=True) + EPS) * norm_gain).astype(jnp.bfloat16)
    normed = jnp.pad(normed.reshape(own, width), ((0, 8 - own), (0, 0)))
    normed = gather(normed, devices, 0).reshape(devices * 8, width)
    real = lambda v: v.reshape(devices, 8, v.shape[1])[:, :own].reshape(rows, v.shape[1])
    q = (jnp.dot(normed, q_weight, preferred_element_type=jnp.float32) + q_bias).astype(jnp.bfloat16)
    kv = jnp.dot(normed, kv_weight.reshape(width, 2 * kv_cols), preferred_element_type=jnp.float32)
    kv = (kv + kv_bias.reshape(2 * kv_cols)).astype(jnp.bfloat16)
    q, kv = real(q), real(kv)
    cosine, sine = rope_parts(pos, HEAD_DIM)
    cosine2 = jnp.concatenate([cosine, cosine], 1)
    sine2 = jnp.concatenate([-sine, sine], 1)

    def rotate(v):
        v = v.astype(jnp.float32)
        return (v * cosine2 + jnp.roll(v, HEAD_DIM // 2, axis=-1) * sine2).astype(jnp.bfloat16)

    pieces = [rotate(q[:, h * HEAD_DIM : (h + 1) * HEAD_DIM]) for h in range(heads)] + [kv]
    first = me * rpc
    slot = first + jnp.arange(rpc, dtype=jnp.int32)
    lanc = lax.dynamic_slice_in_dim(anc, my_prompt * ppr, ppr, 0)
    lmade = lax.dynamic_slice_in_dim(made, my_prompt * ppr, ppr, 1)
    own_lens = lax.dynamic_slice_in_dim(tail_lens, first, rpc, 0)
    t_ok = (lanc[:, None] == slot[None, :])[:, :, None] & (
        jnp.arange(tail, dtype=jnp.int32)[None, None, :] < own_lens[None, :, None]
    )
    f_ok = lmade.T[:, :, None] == slot[None, None, :]
    lok = jnp.concatenate([t_ok.reshape(ppr, rpc * tail), f_ok.reshape(ppr, own)], 1).astype(jnp.float32)
    lok = jnp.pad(lok, ((0, 0), (0, 128 - own)))
    pok = (me * slab + jnp.arange(slab, dtype=jnp.int32))[None, :] < prefix_lens[:, None]
    pok = jnp.broadcast_to(pok.astype(jnp.float32)[:, None], (prompts, 8, slab))
    my_cos = jnp.pad(lax.dynamic_slice_in_dim(cosine2, me * own, own, 0), ((0, 16 - own), (0, 0)))
    my_sin = jnp.pad(lax.dynamic_slice_in_dim(sine2, me * own, own, 0), ((0, 16 - own), (0, 0)))
    pool_hot = prefix_index[:, None] == jnp.arange(prefix_key_cache.shape[0], dtype=jnp.int32)[None, :]
    num, stats = gather_and_attend(
        jnp.stack(pieces, 0),
        jnp.broadcast_to(pool_hot.astype(jnp.float32)[:, :, None, None], pool_hot.shape + (8, HEAD_DIM)),
        prefix_key_cache,
        prefix_value_cache,
        tail_key_cache.reshape(rpc * tail, -1),
        tail_value_cache.reshape(rpc * tail, -1),
        pok, lok, my_cos, my_sin, own, score_scale, devices, 1,
    )
    out = merge_and_project(num, stats, o_weight, heads, rows, 2)
    out = out.reshape(devices, STEPS, rpc, out.shape[1])
    return jnp.transpose(out, (1, 0, 2, 3)).reshape(STEPS, devices * rpc, out.shape[3])


def solution(mesh):
    return jax.shard_map(
        local,
        mesh=mesh,
        in_specs=(
            P(None, ("grp", "beam"), None),
            P(),
            P(None, "beam"),
            P("beam"),
            P(None, None, "beam"),
            P(None, "beam"),
            P(None, "beam"),
            P("grp", "beam", None),
            P("grp", "beam", None),
            P("grp"),
            P("grp"),
            P(("grp", "beam"), None, None),
            P(("grp", "beam"), None, None),
            P("grp"),
            P(None, "grp"),
        ),
        out_specs=P(None, "grp", "beam"),
        check_vma=False,
    )
```
